512 devices in a mesh: expert: 8 (over z), dp: 16 (over y, core), section: 4 (over x).
Axes of the slice: x: 4, y: 8, z: 8, core: 2. Of those that a mesh axis runs over, the one named last changes fastest.
Arguments:
- active: bfloat16 [4, 4096, 2, 8192], P('section', ('expert', 'dp')), may hold values from -6 to 6
- out_grad: bfloat16 [4, 4096, 3072], P('section', ('expert', 'dp')), may hold values from -6 to 6
- proj_model: bfloat16 [64, 3072], P(None, 'dp'), may hold values from -0.109375 to 0.109375
- routes: int32 [4, 4096, 2], P('section', ('expert', 'dp')), may hold values from 0 to 7, all different within a row; in each aligned block of 32 rows (0 to 31, 32 to 63, ..., all dimensions but the last counted through in order) at most 16 rows name the same one
- route_weight: float32 [4, 4096, 2], P('section', ('expert', 'dp')), may hold values from 0.2 to 1
- seq_ids: int32 [4096], P(('expert', 'dp')), may hold values from 0 to 63, never falling along the last dimension, each value on 1 to 128 neighbouring positions
- proj_hidden: bfloat16 [8, 64, 8192], P('expert', None, 'dp'), may hold values from -0.0625 to 0.0625
- query_feat: bfloat16 [4, 8, 256, 4096], P('section', 'expert', 'dp'), may hold values from -0.00390625 to 0.00390625
Outputs:
- scores: float32 [64, 256], P(('expert', 'section'), 'dp')
The draws below stay inside these ranges and needn't reach their ends.
Inputs may be any that keep to these rules, and one draw needn't show every extreme that they name: `routes`: each row names 2 different experts; among the 32 rows of one device at one checkpoint no expert is named by more than 16 rows, and in some device's rows one expert is named by exactly 16 rows. `seq_ids`: sequence numbers never fall along the tokens; each sequence has 1 to 128 tokens, one exactly 128.
All inputs are finite; a program needn't handle non-finite values.
Results may differ from the reference program's by a relative error of at most 0.0029.
Values may be sent and summed in bfloat16 or wider, within the bound.
No kernel may reach another device: no remote copies, remote signals or barrier semaphores. Data moves between devices by JAX's collectives and lax.ppermute only.
A program may use at most 64 MiB of HBM per device.

```python
import math
import jax
import jax.numpy as jnp
import numpy as np
from jax import lax

D = 3072
FF = 8192
EXPERTS = 8
TOP = 2
RANK = 64
QUERIES = 256
SEQS = 64
CKPT = 4
TOK_DEV = 32
TOKENS = 4096
SEQ_MOST = 128
CAP = 16
N_EXPERT = 8
N_DP = 16
N_SECTION = 4


def levels(key, dims, cuts, low, largest):
    def one(position, parts):
        steps = jax.random.uniform(jax.random.fold_in(jax.random.fold_in(key, 6), position), (parts,), jnp.float32, low / len(cuts), largest / len(cuts))
        return jnp.repeat(jnp.exp(steps), dims[position] // parts).reshape((-1,) + (1,) * (len(dims) - position - 1))

    loudness = one(*cuts[0])
    for cut in cuts[1:]:
        loudness = loudness * one(*cut)
    return loudness


def length_profile(count, total, reach, lean):
    weights = [(1 << 20) // math.isqrt(standing ** lean) + 1 for standing in range(2, count + 1)]
    rest, holding = total - reach - (count - 1), [1] * (count - 1)
    while rest > 0:
        movable = [i for i in range(count - 1) if holding[i] < reach]
        mass, remaining = sum([weights[i] for i in movable]), rest
        for i in movable:
            extra = min(reach - holding[i], max(1, remaining * weights[i] // mass), rest)
            holding[i] = holding[i] + extra
            rest = rest - extra
    return np.array([reach] + holding)


def ragged(stream_key, number_of, total, bound, skew):
    if number_of == 2:
        one = jax.random.randint(stream_key, (), max(1, total - bound), min(bound, total - 1) + 1)
        return jnp.stack([one, total - one])
    sizes = jnp.asarray(length_profile(number_of, total, bound, skew), jnp.int32)
    twos = (number_of - 1) // 2
    source_of, taker = sizes[1:1 + 2 * twos:2], sizes[2:2 + 2 * twos:2]
    slack = jnp.minimum(source_of - 1, bound - taker)
    shifted = jax.random.randint(jax.random.fold_in(stream_key, 1), (twos,), 0, 1 << 20) % (slack + 1)
    sizes = sizes.at[1:1 + 2 * twos:2].set(source_of - shifted).at[2:2 + 2 * twos:2].set(taker + shifted)
    return sizes[jax.random.permutation(jax.random.fold_in(stream_key, 2), number_of)]


def assign_block(key, own, number, rows, amount, top, limit, skew):
    order = jax.random.permutation(key, amount)
    crowded, usual = portions_of(amount, rows * top, limit, skew, True), portions_of(amount, rows * top, limit, skew, False)
    places = jnp.arange(amount)

    def named(tallies, turn):
        used = int((tallies > 0).sum())
        fixed = max(1, used // 4)
        shifted = fixed + (places - fixed + turn * (used - fixed)) % max(1, amount - fixed)
        return jnp.zeros((amount,), jnp.int32).at[order[jnp.where(places < fixed, places, shifted)]].set(jnp.asarray(tallies, jnp.int32))

    tallies = jnp.where(number % 4 == 0, named(crowded, number // 4), named(usual, number - number // 4 - 1))
    mixed = jax.random.permutation(jax.random.fold_in(own, 3), amount)
    source_of, taker = mixed[0:amount // 2 * 2:2], mixed[1:amount // 2 * 2:2]
    margin = jnp.minimum(tallies[source_of] - 1, limit - tallies[taker]) // 2
    margin = jnp.where((source_of == order[0]) | (taker == order[0]) | (tallies[taker] == 0), 0, jnp.maximum(margin, 0))
    shifted = jax.random.randint(jax.random.fold_in(own, 4), (amount // 2,), 0, 1 << 20) % (margin + 1)
    tallies = tallies.at[source_of].add(-shifted).at[taker].add(shifted)
    items = jnp.searchsorted(jnp.cumsum(tallies), jnp.arange(rows * top), side="right").astype(jnp.int32)
    listing = items.reshape(top, rows).T
    listing = listing[jax.random.permutation(jax.random.fold_in(own, 1), rows)]
    turn = jax.random.randint(jax.random.fold_in(own, 2), (rows, 1), 0, top)
    return jnp.take_along_axis(listing, (jnp.arange(top)[None, :] + turn) % top, axis=1)


def portions_of(amount, total, bound, slope, full):
    portions = [(1 << 20) // math.isqrt(rank ** slope) + 1 for rank in range(1, amount + 1)]
    largest = bound if full else min(bound, max(-(-total // amount), total * portions[0] // sum(portions)))
    least = 1 if total - largest >= amount - 1 else 0
    given, surplus = [largest] + [least] * (amount - 1), total - largest - least * (amount - 1)
    while surplus > 0:
        free = [i for i in range(1, amount) if given[i] < largest] or [i for i in range(1, amount) if given[i] < bound]
        whole, left = sum([portions[i] for i in free]), surplus
        for i in free:
            addition = min(bound - given[i], max(1, left * portions[i] // whole), surplus)
            given[i] = given[i] + addition
            surplus = surplus - addition
    return np.array(given)


def gaussian(stream_key, shape, width, reach, cuts=(), held_as=jnp.bfloat16):
    array = width * jax.random.normal(stream_key, shape, jnp.float32)
    if cuts:
        array = array * levels(stream_key, shape, cuts, -0.22, 0.18)
    return jnp.clip(array, -reach, reach).astype(held_as)


def setup_inputs(seed: int = 0) -> dict:
    splits = jax.random.split(jax.random.key(seed), 9)
    active = gaussian(splits[0], (CKPT, TOKENS, TOP, FF), 1.0, 6.0, ((0, 4), (1, 128)))
    out_grad = gaussian(splits[1], (CKPT, TOKENS, D), 1.0, 6.0, ((0, 4), (1, 128)))
    proj_model = gaussian(splits[2], (RANK, D), D ** -0.5, 0.109375, ((1, 16),))
    routes_keys = jax.random.split(jax.random.fold_in(splits[3], 1), CKPT * TOKENS // TOK_DEV)
    routes_turns = jax.random.permutation(jax.random.fold_in(splits[3], 3), CKPT * TOKENS // TOK_DEV)
    routes = jax.vmap(lambda own, number: assign_block(jax.random.fold_in(splits[3], 2), own, number, TOK_DEV, EXPERTS, TOP, CAP, 2))(routes_keys, routes_turns).reshape((CKPT, TOKENS, TOP))
    route_weight = jnp.clip(0.2 + 0.8 * jax.random.uniform(splits[4], (CKPT, TOKENS, TOP), jnp.float32) ** levels(splits[4], (CKPT, TOKENS, TOP), ((0, 4), (1, 128)), -0.2, 0.2), 0.2, 1.0)
    seq_ids = jnp.searchsorted(jnp.cumsum(ragged(splits[5], SEQS, TOKENS, SEQ_MOST, 1)), jnp.arange(TOKENS), side="right").astype(jnp.int32)
    proj_hidden = gaussian(splits[6], (EXPERTS, RANK, FF), FF ** -0.5, 0.0625, ((0, 8), (2, 16)))
    query_feat = gaussian(splits[7], (CKPT, EXPERTS, QUERIES, RANK * RANK), (RANK * RANK * TOKENS * TOP * N_SECTION // SEQS) ** -0.5, 0.00390625, ((0, 4), (1, 8), (2, 16)))
    return dict(active=active, out_grad=out_grad, proj_model=proj_model, routes=routes, route_weight=route_weight, seq_ids=seq_ids, proj_hidden=proj_hidden, query_feat=query_feat)


def reference(active, out_grad, proj_model, routes, route_weight, seq_ids, proj_hidden, query_feat):
    hold = min(TOKENS * TOP, N_EXPERT * N_DP * CAP)
    labels = jnp.arange(SEQS, dtype=jnp.int32)
    seq_flat = jnp.repeat(seq_ids, TOP)
    expert_ids = jnp.arange(EXPERTS, dtype=jnp.int32)

    def one_ckpt(ckpt):
        dy_proj = jnp.dot(out_grad[ckpt], proj_model.T, preferred_element_type=jnp.float32)
        scaled = (route_weight[ckpt][:, :, None] * dy_proj[:, None, :]).astype(jnp.bfloat16)
        flat_routes = routes[ckpt].reshape(-1)
        order = jnp.argsort(flat_routes, stable=True).astype(jnp.int32)
        padded = jnp.concatenate([order, jnp.zeros((hold,), jnp.int32)])
        counts = jnp.sum((flat_routes[:, None] == expert_ids[None, :]).astype(jnp.int32), axis=0).astype(jnp.int32)
        starts = (jnp.cumsum(counts) - counts).astype(jnp.int32)
        act_flat = active[ckpt].reshape(-1, FF)
        vec_flat = scaled.reshape(-1, RANK)
        queries = query_feat[ckpt]

        def one_expert(expert_id):
            pick = lax.dynamic_slice_in_dim(padded, starts[expert_id], hold)
            valid = jnp.arange(hold, dtype=jnp.int32) < counts[expert_id]
            rows = act_flat[pick]
            act_proj = jnp.dot(rows, proj_hidden[expert_id].T, preferred_element_type=jnp.float32)
            vectors = jnp.where(valid[:, None], vec_flat[pick].astype(jnp.float32), jnp.float32(0.0))
            member = (seq_flat[pick][:, None] == labels[None, :]).astype(jnp.float32)
            outer = (act_proj[:, :, None] * vectors[:, None, :]).reshape(hold, RANK * RANK)
            feature = jnp.dot(member.T, outer, precision=lax.Precision.HIGHEST)
            return jnp.dot(feature, queries[expert_id].astype(jnp.float32).T, precision=lax.Precision.HIGHEST)

        return jnp.sum(lax.map(one_expert, expert_ids), axis=0)

    per_ckpt = lax.map(one_ckpt, jnp.arange(CKPT, dtype=jnp.int32))
    return jnp.sum(per_ckpt, axis=0)
```

```python
import jax
import jax.numpy as jnp
from jax import lax
from jax.experimental import pallas as pl
from jax.experimental.pallas import tpu as pltpu
from jax.sharding import PartitionSpec as P

SEQS = 64
CAP = 16
F32 = jnp.float32
BF16 = jnp.bfloat16


def exchange(x, axes):
    return lax.all_to_all(x, axes, split_axis=0, concat_axis=0, tiled=True)


def dot(a, b, contract=((1,), (0,)), **kw):
    return lax.dot_general(a, b, (contract, ((), ())), preferred_element_type=F32, **kw)


def score_kernel(known_ref, q_ref, out_ref):
    holders, experts, _, lanes = known_ref.shape
    rank = lanes // 2
    queries = q_ref.shape[1] // rank
    wide = q_ref.shape[1]
    row = lax.broadcasted_iota(jnp.int32, (lanes, lanes), 0)
    col = lax.broadcasted_iota(jnp.int32, (lanes, lanes), 1)
    twice = ((row >= rank) & ((row == col) | (row == col + rank))).astype(BF16)
    owner = lax.broadcasted_iota(jnp.int32, (experts, experts * CAP), 1) // CAP
    own = owner == lax.broadcasted_iota(jnp.int32, (experts, experts * CAP), 0)
    label = lax.broadcasted_iota(jnp.int32, (SEQS, experts * CAP), 0).astype(F32)

    def step(d, total):
        block = known_ref[d]
        rows = block[:, :CAP, :].reshape(experts * CAP, lanes)
        line = block[:, CAP, :].astype(F32)
        seqs = jnp.sum(jnp.where(own, line, 0.0), axis=0, keepdims=True)
        temp = dot(rows, q_ref[...])
        vecs = dot(rows, twice)
        prod = jnp.concatenate([temp[:, i : i + lanes] * vecs for i in range(0, wide, lanes)], axis=1)
        high = prod.astype(BF16)
        low = (prod - high.astype(F32)).astype(BF16)
        sel = (label == seqs).astype(F32).astype(BF16)
        return total + (dot(sel, high) + dot(sel, low))

    total = lax.fori_loop(0, holders, step, jnp.zeros((SEQS, wide), F32))
    group = lax.broadcasted_iota(jnp.int32, (wide, lanes), 0) // rank
    ones = (group == lax.broadcasted_iota(jnp.int32, (wide, lanes), 1)).astype(F32)
    out_ref[...] = dot(total, ones, precision=lax.Precision.HIGHEST)[:, :queries]


def on_device(active, out_grad, proj_model, routes, route_weight, seq_ids, proj_hidden, query_feat):
    experts = lax.axis_size("expert")
    holders = lax.axis_size("dp")
    toks, top, hidden = active.shape[1:]
    rank = proj_model.shape[0]
    chunk = hidden // holders
    width = out_grad.shape[2] // holders
    pairs = top * toks
    half = toks // 2

    ids = routes[0].T.reshape(pairs)

    weights = proj_hidden
    order = [0]
    bit = experts // 2
    while bit:
        other = lax.ppermute(weights, "expert", [(i, i ^ bit) for i in range(experts)])
        weights = jnp.concatenate([weights, other], axis=0)
        order = order + [o ^ bit for o in order]
        bit //= 2
    me = lax.axis_index("expert")

    acts = active[0].reshape(toks, top, holders, chunk).transpose(2, 1, 0, 3).reshape(holders, pairs, chunk)
    grads = out_grad[0].reshape(toks, holders, width).transpose(1, 0, 2)
    named = jnp.broadcast_to(routes[0].astype(BF16)[None], (holders, toks, top))
    gap = jnp.zeros((holders, toks, chunk // 2 - width - top), BF16)
    side = jnp.concatenate([grads, named, gap], axis=2)
    side = jnp.concatenate([side[:, :half], side[:, half:]], axis=2)
    got = exchange(jnp.concatenate([acts, side], axis=1), "dp")

    rows = got[:, :pairs].reshape(holders * pairs, chunk)
    every = lax.dot_general(
        rows, weights.reshape(experts * rank, chunk), (((1,), (1,)), ((), ())), preferred_element_type=F32
    )
    rest = jnp.concatenate([got[:, pairs:, : chunk // 2], got[:, pairs:, chunk // 2 :]], axis=1)
    code = rest[:, :, width : width + top].transpose(0, 2, 1).reshape(holders * pairs, 1)
    part = jnp.zeros((holders * pairs, rank), F32)
    for e in range(experts):
        part = part + jnp.where(code == (me ^ order[e]).astype(BF16), every[:, e * rank : (e + 1) * rank], 0.0)
    part_dy = lax.dot_general(
        rest[:, :, :width], proj_model, (((2,), (1,)), ((), ())), preferred_element_type=F32
    )
    part = part.reshape(holders, top, toks, rank)
    send = jnp.concatenate(
        [
            jnp.concatenate([part[:, 0], part[:, 1]], axis=2),
            jnp.concatenate([part_dy[:, :half], part_dy[:, half:]], axis=2),
        ],
        axis=1,
    )
    whole = jnp.sum(exchange(send, "dp"), axis=0)
    act_proj = jnp.concatenate([whole[:toks, :rank], whole[:toks, rank:]], axis=0)
    dy_proj = jnp.concatenate([whole[toks:, :rank], whole[toks:, rank:]], axis=0)
    scaled = (route_weight[0].T[:, :, None] * dy_proj[None]).astype(BF16).reshape(pairs, rank)

    member = (ids[:, None] == jnp.arange(experts)[None, :]).astype(F32)
    before = lax.dot_general(
        jnp.tril(jnp.ones((pairs, pairs), F32), -1), member, (((1,), (0,)), ((), ())), preferred_element_type=F32
    )
    place = jnp.sum(before * member, axis=1)
    slot = ids * CAP + place.astype(jnp.int32)
    pick = (jnp.arange(experts * CAP)[:, None] == slot[None, :]).astype(BF16)
    both = jnp.concatenate([act_proj.astype(BF16), scaled], axis=1)
    slots = lax.dot_general(pick, both, (((1,), (0,)), ((), ())), preferred_element_type=F32).astype(BF16)
    pair_seq = jnp.concatenate([seq_ids] * top).astype(BF16)
    belongs = (place[:, None].astype(jnp.int32) == (jnp.arange(2 * rank) % CAP)[None, :]).astype(BF16)
    line = dot((member * jnp.concatenate([seq_ids] * top)[:, None].astype(F32)).astype(BF16), belongs, ((0,), (0,)))
    line = jnp.pad(line.astype(BF16)[:, None], ((0, 0), (0, 7), (0, 0)))
    moved = exchange(jnp.concatenate([slots.reshape(experts, CAP, 2 * rank), line], axis=1), "expert")
    known = lax.all_gather(moved, "dp", axis=0, tiled=False)

    queries = query_feat.shape[2]
    q = query_feat[0, 0].reshape(queries, rank, rank).transpose(1, 0, 2).reshape(rank, queries * rank)
    q = jnp.pad(q, ((0, rank), (0, 0)))
    scores = pl.pallas_call(
        score_kernel,
        out_shape=jax.ShapeDtypeStruct((SEQS, queries), F32),
        in_specs=[pl.BlockSpec(memory_space=pltpu.VMEM)] * 2,
        out_specs=pl.BlockSpec(memory_space=pltpu.VMEM),
        name="score",
    )(known, q)
    sections = lax.axis_size("section")
    out = exchange(scores.reshape(experts * sections, SEQS // (experts * sections), queries), ("expert", "section"))
    return jnp.sum(out, axis=0)


def solution(mesh):
    placed = (
        P("section", ("expert", "dp"), None, None),
        P("section", ("expert", "dp"), None),
        P(None, "dp"),
        P("section", ("expert", "dp"), None),
        P("section", ("expert", "dp"), None),
        P(("expert", "dp")),
        P("expert", None, "dp"),
        P("section", "expert", "dp", None),
    )
    return jax.shard_map(
        on_device,
        mesh=mesh,
        in_specs=placed,
        out_specs=P(("expert", "section"), "dp"),
        check_vma=False,
    )
```

```python
import jax
import jax.numpy as jnp
from jax import lax
from jax.experimental import pallas as pl
from jax.experimental.pallas import tpu as pltpu
from jax.sharding import PartitionSpec as P

SEQS = 64
CAP = 16
LANES = 128
ROOM = 20 << 20
F32 = jnp.float32
BF16 = jnp.bfloat16
VMEM = pl.BlockSpec(memory_space=pltpu.VMEM)
SMEM = pl.BlockSpec(memory_space=pltpu.SMEM)


def exchange(x, axes):
    return lax.all_to_all(x, axes, split_axis=0, concat_axis=0, tiled=True)


def dot(a, b, contract=((1,), (0,)), **kw):
    return lax.dot_general(a, b, (contract, ((), ())), preferred_element_type=F32, **kw)


def iota(shape, axis):
    return lax.broadcasted_iota(jnp.int32, shape, axis)


def call(kernel, name, shape, dtype, *args):
    specs = [SMEM if a.ndim == 1 else VMEM for a in args]
    return pl.pallas_call(
        kernel,
        name=name,
        out_shape=jax.ShapeDtypeStruct(shape, dtype),
        in_specs=specs,
        out_specs=VMEM,
        compiler_params=pltpu.CompilerParams(vmem_limit_bytes=ROOM),
    )(*args)


def pack_kernel(acts_ref, grads_ref, routes_ref, out_ref):
    holders, _, chunk = out_ref.shape
    pairs = acts_ref.shape[0]
    toks, feats = grads_ref.shape
    width = feats // holders
    half = toks // 2
    token, lane = iota((toks, LANES), 0), iota((toks, LANES), 1) % pairs
    named = routes_ref[...].astype(F32).astype(BF16)
    first = dot(named, (lane == 2 * token).astype(F32).astype(BF16))
    second = dot(named, (lane == 2 * token + 1).astype(F32).astype(BF16))
    code = jnp.broadcast_to(first[0:1] + second[1:2], (toks, LANES))
    low = iota((toks, LANES), 1) < width % LANES
    for j in range(holders):
        out_ref[j, :pairs, :] = acts_ref[:, j * chunk : (j + 1) * chunk]
        base = width * j // LANES * LANES
        left = grads_ref[:, base : base + LANES]
        right = grads_ref[:, base + LANES : base + 2 * LANES]
        if width * j == base:
            right = jnp.where(low, right.astype(F32), code).astype(BF16)
        else:
            left = jnp.where(low, code, left.astype(F32)).astype(BF16)
        for k in range(2):
            rows = slice(k * half, (k + 1) * half)
            out_ref[j, pairs:, 2 * k * LANES : (2 * k + 1) * LANES] = left[rows]
            out_ref[j, pairs:, (2 * k + 1) * LANES : (2 * k + 2) * LANES] = right[rows]


def project_kernel(odd_ref, order_ref, got_ref, weights_ref, model_ref, out_ref):
    holders, rows, chunk = got_ref.shape
    rank = LANES // 2
    pairs = rank
    half = pairs // 2
    experts = weights_ref.shape[0] // rank
    odd = odd_ref[0] == 1
    low = iota((half, LANES), 1) < rank
    left = got_ref[:, pairs, 0:LANES].astype(F32)
    right = got_ref[:, pairs, LANES : 2 * LANES].astype(F32)
    code = jnp.where(odd, left, pltpu.roll(right, rank, 1))
    code = jnp.transpose(code)
    lane = iota((1, LANES), 1)
    wanted = [
        jnp.where(lane < rank, order_ref[2 * m], order_ref[2 * m + 1]).astype(F32) for m in range(experts // 2)
    ]
    part = 4
    for g in range(0, holders, part):
        every = dot(
            got_ref[g : g + part, :pairs, :].reshape(part * pairs, chunk), weights_ref[...], ((1,), (1,))
        )
        for h in range(part):
            col = jnp.broadcast_to(code[:pairs, g + h : g + h + 1], (pairs, LANES))
            own = jnp.zeros((pairs, LANES), F32)
            for m in range(experts // 2):
                block = every[h * pairs : (h + 1) * pairs, m * LANES : (m + 1) * LANES]
                own = own + jnp.where(col == wanted[m], block, 0.0)
            own = own + pltpu.roll(own, rank, 1)
            out_ref[g + h, :half, :] = jnp.where(low, own[:half], own[half:])
    side = rows - pairs
    begin = dot(got_ref[:, pairs:, : chunk // 2].reshape(holders * side, chunk // 2), model_ref[...], ((1,), (1,)))
    end = dot(got_ref[:, pairs:, chunk // 2 :].reshape(holders * side, chunk // 2), model_ref[...], ((1,), (1,)))
    both = jnp.where(iota((holders * side, LANES), 1) < rank, begin, end)
    out_ref[:, half:, :] = both.reshape(holders, side, LANES)


def slots_kernel(parts_ref, weight_ref, pick_ref, line_ref, out_ref):
    holders, rows, _ = parts_ref.shape
    experts = out_ref.shape[0]
    rank = LANES // 2
    toks = weight_ref.shape[0]
    whole = parts_ref[0]
    for h in range(1, holders):
        whole = whole + parts_ref[h]
    low = iota((toks, LANES), 1) < rank
    acts, dy = whole[:toks], whole[toks:]
    dy = jnp.concatenate([pltpu.roll(dy, rank, 1), dy], axis=0)
    table = jnp.concatenate(
        [
            jnp.where(low, acts, 0.0),
            jnp.where(low, pltpu.roll(acts, rank, 1), 0.0),
            jnp.where(low, 0.0, weight_ref[:, 0:1] * dy),
            jnp.where(low, 0.0, weight_ref[:, 1:2] * dy),
        ],
        axis=0,
    )
    slots = dot(pick_ref[...], table.astype(BF16)).astype(BF16)
    out_ref[:, :CAP, :] = slots.reshape(experts, CAP, LANES)
    first = iota((experts, 8, LANES), 1) == 0
    out_ref[:, CAP:, :] = jnp.where(first, line_ref[...][:, None, :], 0.0).astype(BF16)


def score_kernel(known_ref, q_ref, out_ref, sums_ref):
    holders, rows, lanes = known_ref.shape
    rank, wide = q_ref.shape
    queries = wide // rank
    per = lanes // queries
    slots = rows - 8
    spread_row, spread_col = iota((rank, lanes), 0), iota((rank, lanes), 1) // queries
    blank = jnp.zeros((rank, lanes), BF16)
    part = 8
    label = iota((SEQS, slots), 0).astype(F32)
    total = jnp.zeros((SEQS, 2 * lanes), F32)
    for g in range(0, holders, part):
        lhs = known_ref[g : g + part, :slots, :].reshape(part * slots, lanes)
        for c in range(wide // lanes):
            spread = (spread_row == c * per + spread_col).astype(F32).astype(BF16)
            top = jnp.concatenate([q_ref[:, c * lanes : (c + 1) * lanes], blank], axis=1)
            rhs = jnp.concatenate([top, jnp.concatenate([blank, spread], axis=1)], axis=0)
            both = dot(lhs, rhs)
            prod = both[:, :lanes] * both[:, lanes:]
            if c == 0:
                sums_ref[...] = prod
            else:
                sums_ref[...] += prod
        sums = sums_ref[...]
        high = sums.astype(BF16)
        low = (sums - high.astype(F32)).astype(BF16)
        seqs = known_ref[g : g + part, slots, :].astype(F32)
        sel = jnp.concatenate(
            [(label == seqs[i : i + 1]).astype(F32).astype(BF16) for i in range(part)], axis=1
        )
        total = total + dot(sel, jnp.concatenate([high, low], axis=1))
    score = total[:, :lanes] + total[:, lanes:]
    step = lanes // 2
    while step >= queries:
        score = score + pltpu.roll(score, step, 1)
        step //= 2
    out_ref[...] = score[:, :queries]


def on_device(active, out_grad, proj_model, routes, route_weight, seq_ids, proj_hidden, query_feat):
    experts = lax.axis_size("expert")
    sections = lax.axis_size("section")
    holders = lax.axis_size("dp")
    toks, top, hidden = active.shape[1:]
    rank, width = proj_model.shape
    chunk = hidden // holders
    pairs = top * toks
    me = lax.axis_index("expert")
    odd = lax.axis_index("dp") % 2

    sent = call(
        pack_kernel, "pack", (holders, pairs + toks // 2, chunk), BF16,
        active[0].reshape(pairs, hidden), out_grad[0], routes[0].T,
    )
    got = exchange(sent, "dp")

    weights = proj_hidden
    order = [0]
    bit = experts // 2
    while bit:
        other = lax.ppermute(weights, "expert", [(i, i ^ bit) for i in range(experts)])
        weights = jnp.concatenate([weights, other], axis=0)
        order = order + [o ^ bit for o in order]
        bit //= 2
    named = me ^ jnp.array(order, jnp.int32)
    gap = 2 * LANES - width
    model = jnp.where(
        odd == 1, jnp.pad(proj_model, ((0, 0), (gap, 0))), jnp.pad(proj_model, ((0, 0), (0, gap)))
    )
    model = jnp.concatenate([model, model], axis=0)
    partial = call(
        project_kernel, "project", (holders, toks + toks // 2, LANES), F32,
        odd.reshape(1), named, got, weights.reshape(experts * rank, chunk), model,
    )
    parts = exchange(partial, "dp")

    ids = routes[0].reshape(pairs)
    member = (ids[:, None] == jnp.arange(experts)[None, :]).astype(BF16)
    before = dot(jnp.tril(jnp.ones((pairs, pairs), BF16), -1), member)
    place = jnp.sum(before * member.astype(F32), axis=1).astype(jnp.int32)
    slot = ids * CAP + place
    slot = jnp.concatenate([slot, slot.reshape(toks, top).T.reshape(pairs)])
    pick = (jnp.arange(experts * CAP)[:, None] == slot[None, :]).astype(BF16)
    belongs = (place[:, None] == (jnp.arange(LANES) % CAP)[None, :]).astype(BF16)
    pair_seq = jnp.repeat(seq_ids, top).astype(BF16)
    line = dot(member * pair_seq[:, None], belongs, ((0,), (0,)))
    slots = call(
        slots_kernel, "slots", (experts, CAP + 8, LANES), BF16, parts, route_weight[0], pick, line
    )
    moved = exchange(slots, "expert")
    own = jnp.arange(LANES)[None, :] // CAP == jnp.arange(experts)[:, None]
    seqs = jnp.sum(jnp.where(own, moved[:, CAP, :].astype(F32), 0.0), axis=0).astype(BF16)
    mine = jnp.concatenate(
        [moved[:, :CAP].reshape(experts * CAP, LANES), jnp.broadcast_to(seqs[None], (8, LANES))], axis=0
    )
    known = lax.all_gather(mine, "dp", axis=0, tiled=False)

    queries = query_feat.shape[2]
    q = query_feat[0, 0].reshape(queries, rank, rank).transpose(1, 2, 0).reshape(rank, rank * queries)
    scores = pl.pallas_call(
        score_kernel,
        name="score",
        out_shape=jax.ShapeDtypeStruct((SEQS, queries), F32),
        in_specs=[VMEM] * 2,
        out_specs=VMEM,
        scratch_shapes=[pltpu.VMEM((8 * experts * CAP, LANES), F32)],
        compiler_params=pltpu.CompilerParams(vmem_limit_bytes=ROOM),
    )(known, q)
    out = exchange(scores.reshape(experts * sections, SEQS // (experts * sections), queries), ("expert", "section"))
    return jnp.sum(out, axis=0)


def solution(mesh):
    placed = (
        P("section", ("expert", "dp"), None, None),
        P("section", ("expert", "dp"), None),
        P(None, "dp"),
        P("section", ("expert", "dp"), None),
        P("section", ("expert", "dp"), None),
        P(("expert", "dp")),
        P("expert", None, "dp"),
        P("section", "expert", "dp", None),
    )
    return jax.shard_map(
        on_device,
        mesh=mesh,
        in_specs=placed,
        out_specs=P(("expert", "section"), "dp"),
        check_vma=False,
    )
```

```python
import jax
import jax.numpy as jnp
from jax import lax
from jax.experimental import pallas as pl
from jax.experimental.pallas import tpu as pltpu
from jax.sharding import PartitionSpec as P

SEQS = 64
CAP = 16
LANES = 128
ROOM = 20 << 20
F32 = jnp.float32
BF16 = jnp.bfloat16
DP = ("y_hi", "y_lo", "core")
GROUP = ("y_lo", "core", "section")
VMEM = pl.BlockSpec(memory_space=pltpu.VMEM)
SMEM = pl.BlockSpec(memory_space=pltpu.SMEM)


def exchange(x, axes):
    return lax.all_to_all(x, axes, split_axis=0, concat_axis=0, tiled=True)


def dot(a, b, contract=((1,), (0,)), **kw):
    return lax.dot_general(a, b, (contract, ((), ())), preferred_element_type=F32, **kw)


def iota(shape, axis):
    return lax.broadcasted_iota(jnp.int32, shape, axis)


def call(kernel, name, shape, dtype, *args):
    specs = [SMEM if a.ndim == 1 else VMEM for a in args]
    return pl.pallas_call(
        kernel,
        name=name,
        out_shape=jax.ShapeDtypeStruct(shape, dtype),
        in_specs=specs,
        out_specs=VMEM,
        compiler_params=pltpu.CompilerParams(vmem_limit_bytes=ROOM),
    )(*args)


def pack_kernel(turn_ref, acts_ref, grads_ref, routes_ref, out_ref):
    holders, _, chunk = out_ref.shape
    pairs = acts_ref.shape[0]
    toks, feats = grads_ref.shape
    width = feats // holders
    half = toks // 2
    token, lane = iota((toks, LANES), 0), iota((toks, LANES), 1) % pairs
    named = routes_ref[...].astype(F32).astype(BF16)
    first = dot(named, (lane == 2 * token).astype(F32).astype(BF16))
    second = dot(named, (lane == 2 * token + 1).astype(F32).astype(BF16))
    code = jnp.broadcast_to(first[0:1] + second[1:2], (toks, LANES))
    low = iota((toks, LANES), 1) < width % LANES
    sections = 4
    spread = holders // sections
    for j in range(holders):
        place, section = j // sections, j % sections
        big = lax.rem(turn_ref[0] + section, sections)
        begin = pl.multiple_of(big * (spread * chunk) + place * chunk, chunk)
        out_ref[j, :pairs, :] = acts_ref[:, pl.ds(begin, chunk)]
        shift = width * place // LANES * LANES
        base = pl.multiple_of(big * (spread * width) + shift, LANES)
        left = grads_ref[:, pl.ds(base, LANES)]
        right = grads_ref[:, pl.ds(pl.multiple_of(base + LANES, LANES), LANES)]
        if width * place == shift:
            right = jnp.where(low, right.astype(F32), code).astype(BF16)
        else:
            left = jnp.where(low, code, left.astype(F32)).astype(BF16)
        for k in range(2):
            rows = slice(k * half, (k + 1) * half)
            out_ref[j, pairs:, 2 * k * LANES : (2 * k + 1) * LANES] = left[rows]
            out_ref[j, pairs:, (2 * k + 1) * LANES : (2 * k + 2) * LANES] = right[rows]


def project_kernel(odd_ref, order_ref, got_ref, model_ref, *refs):
    *weight_refs, out_ref = refs
    holders, rows, chunk = got_ref.shape
    rank = LANES // 2
    pairs = rank
    half = pairs // 2
    experts = len(weight_refs)
    weights = jnp.concatenate([ref[...] for ref in weight_refs], axis=0)
    model = jnp.concatenate([model_ref[...]] * 2, axis=0)
    odd = odd_ref[0] == 1
    low = iota((half, LANES), 1) < rank
    left = got_ref[:, pairs, 0:LANES].astype(F32)
    right = got_ref[:, pairs, LANES : 2 * LANES].astype(F32)
    code = jnp.where(odd, left, pltpu.roll(right, rank, 1))
    code = jnp.transpose(code)
    lane = iota((1, LANES), 1)
    wanted = [
        jnp.where(lane < rank, order_ref[2 * m], order_ref[2 * m + 1]).astype(F32) for m in range(experts // 2)
    ]
    part = 4
    for g in range(0, holders, part):
        every = dot(
            got_ref[g : g + part, :pairs, :].reshape(part * pairs, chunk), weights, ((1,), (1,))
        )
        for h in range(part):
            col = jnp.broadcast_to(code[:pairs, g + h : g + h + 1], (pairs, LANES))
            own = jnp.zeros((pairs, LANES), F32)
            for m in range(experts // 2):
                block = every[h * pairs : (h + 1) * pairs, m * LANES : (m + 1) * LANES]
                own = own + jnp.where(col == wanted[m], block, 0.0)
            own = own + pltpu.roll(own, rank, 1)
            out_ref[g + h, :half, :] = jnp.where(low, own[:half], own[half:])
    side = rows - pairs
    begin = dot(got_ref[:, pairs:, : chunk // 2].reshape(holders * side, chunk // 2), model, ((1,), (1,)))
    end = dot(got_ref[:, pairs:, chunk // 2 :].reshape(holders * side, chunk // 2), model, ((1,), (1,)))
    both = jnp.where(iota((holders * side, LANES), 1) < rank, begin, end)
    out_ref[:, half:, :] = both.reshape(holders, side, LANES)


def slots_kernel(parts_ref, weight_ref, pick_ref, line_ref, out_ref):
    holders, rows, _ = parts_ref.shape
    experts = out_ref.shape[0]
    rank = LANES // 2
    toks = weight_ref.shape[0]
    whole = parts_ref[0]
    for h in range(1, holders):
        whole = whole + parts_ref[h]
    low = iota((toks, LANES), 1) < rank
    acts, dy = whole[:toks], whole[toks:]
    dy = jnp.concatenate([pltpu.roll(dy, rank, 1), dy], axis=0)
    table = jnp.concatenate(
        [
            jnp.where(low, acts, 0.0),
            jnp.where(low, pltpu.roll(acts, rank, 1), 0.0),
            jnp.where(low, 0.0, weight_ref[:, 0:1] * dy),
            jnp.where(low, 0.0, weight_ref[:, 1:2] * dy),
        ],
        axis=0,
    )
    slots = dot(pick_ref[...], table.astype(BF16)).astype(BF16)
    out_ref[:, :CAP, :] = slots.reshape(experts, CAP, LANES)
    first = iota((experts, 8, LANES), 1) == 0
    out_ref[:, CAP:, :] = jnp.where(first, line_ref[...][:, None, :], 0.0).astype(BF16)


def score_kernel(known_ref, q_ref, out_ref, sums_ref):
    holders, rows, lanes = known_ref.shape
    rank, wide = q_ref.shape
    queries = wide // rank
    per = lanes // queries
    slots = rows - 8
    spread_row, spread_col = iota((rank, lanes), 0), iota((rank, lanes), 1) // queries
    blank = jnp.zeros((rank, lanes), BF16)
    part = 8
    label = iota((SEQS, slots), 0).astype(F32)
    total = jnp.zeros((SEQS, 2 * lanes), F32)
    for g in range(0, holders, part):
        lhs = known_ref[g : g + part, :slots, :].reshape(part * slots, lanes)
        for c in range(wide // lanes):
            spread = (spread_row == c * per + spread_col).astype(F32).astype(BF16)
            top = jnp.concatenate([q_ref[:, c * lanes : (c + 1) * lanes], blank], axis=1)
            rhs = jnp.concatenate([top, jnp.concatenate([blank, spread], axis=1)], axis=0)
            both = dot(lhs, rhs)
            prod = both[:, :lanes] * both[:, lanes:]
            if c == 0:
                sums_ref[...] = prod
            else:
                sums_ref[...] += prod
        sums = sums_ref[...]
        high = sums.astype(BF16)
        low = (sums - high.astype(F32)).astype(BF16)
        seqs = known_ref[g : g + part, slots, :].astype(F32)
        sel = jnp.concatenate(
            [(label == seqs[i : i + 1]).astype(F32).astype(BF16) for i in range(part)], axis=1
        )
        total = total + dot(sel, jnp.concatenate([high, low], axis=1))
    score = total[:, :lanes] + total[:, lanes:]
    step = lanes // 2
    while step >= queries:
        score = score + pltpu.roll(score, step, 1)
        step //= 2
    out_ref[...] = score[:, :queries]


def on_device(active, out_grad, proj_model, routes, route_weight, seq_ids, proj_hidden, query_feat):
    experts = lax.axis_size("expert")
    sections = lax.axis_size("section")
    holders = lax.axis_size(DP)
    toks, top, hidden = active.shape[1:]
    rank, width = proj_model.shape
    chunk = hidden // holders
    pairs = top * toks
    me = lax.axis_index("expert")
    odd = lax.axis_index("core")
    turns = lax.axis_size("y_hi")

    sent = call(
        pack_kernel, "pack", (holders, pairs + toks // 2, chunk), BF16,
        lax.axis_index("y_hi").reshape(1), active[0].reshape(pairs, hidden), out_grad[0], routes[0].T,
    )
    got = exchange(sent, GROUP)

    gap = 2 * LANES - width
    model = jnp.where(
        odd == 1, jnp.pad(proj_model, ((0, 0), (gap, 0))), jnp.pad(proj_model, ((0, 0), (0, gap)))
    )
    tied = jnp.concatenate([proj_hidden[0], model], axis=1)
    moves = [
        ((section + y) % turns * sections + section, y * sections + section)
        for y in range(turns)
        for section in range(sections)
    ]
    tied = lax.ppermute(tied, ("y_hi", "section"), moves)
    weights, model = tied[:, :chunk], tied[:, chunk:]
    weights = [weights] + [
        lax.ppermute(weights, "expert", [(i, (i + k) % experts) for i in range(experts)]) for k in range(1, experts)
    ]
    named = (me + experts - jnp.arange(experts, dtype=jnp.int32)) % experts
    partial = call(
        project_kernel, "project", (holders, toks + toks // 2, LANES), F32,
        odd.reshape(1), named, got, model, *weights,
    )
    parts = exchange(partial, GROUP)

    ids = routes[0].reshape(pairs)
    member = (ids[:, None] == jnp.arange(experts)[None, :]).astype(BF16)
    before = dot(jnp.tril(jnp.ones((pairs, pairs), BF16), -1), member)
    place = jnp.sum(before * member.astype(F32), axis=1).astype(jnp.int32)
    slot = ids * CAP + place
    slot = jnp.concatenate([slot, slot.reshape(toks, top).T.reshape(pairs)])
    pick = (jnp.arange(experts * CAP)[:, None] == slot[None, :]).astype(BF16)
    belongs = (place[:, None] == (jnp.arange(LANES) % CAP)[None, :]).astype(BF16)
    pair_seq = jnp.repeat(seq_ids, top).astype(BF16)
    line = dot(member * pair_seq[:, None], belongs, ((0,), (0,)))
    slots = call(
        slots_kernel, "slots", (experts, CAP + 8, LANES), BF16, parts, route_weight[0], pick, line
    )
    moved = exchange(slots, "expert")
    own = jnp.arange(LANES)[None, :] // CAP == jnp.arange(experts)[:, None]
    seqs = jnp.sum(jnp.where(own, moved[:, CAP, :].astype(F32), 0.0), axis=0).astype(BF16)
    mine = jnp.concatenate(
        [moved[:, :CAP].reshape(experts * CAP, LANES), jnp.broadcast_to(seqs[None], (8, LANES))], axis=0
    )
    known = lax.all_gather(mine, DP, axis=0, tiled=False)

    queries = query_feat.shape[2]
    q = query_feat[0, 0].reshape(queries, rank, rank).transpose(1, 2, 0).reshape(rank, rank * queries)
    scores = pl.pallas_call(
        score_kernel,
        name="score",
        out_shape=jax.ShapeDtypeStruct((SEQS, queries), F32),
        in_specs=[VMEM] * 2,
        out_specs=VMEM,
        scratch_shapes=[pltpu.VMEM((8 * experts * CAP, LANES), F32)],
        compiler_params=pltpu.CompilerParams(vmem_limit_bytes=ROOM),
    )(known, q)
    out = exchange(scores.reshape(experts * sections, SEQS // (experts * sections), queries), ("expert", "section"))
    return jnp.sum(out, axis=0)


def solution(mesh):
    experts, holders, sections = mesh.devices.shape
    shape = (experts, holders // 4, 2, 2, sections)
    finer = jax.sharding.Mesh(mesh.devices.reshape(shape), ("expert",) + DP + ("section",))
    tokens = ("expert",) + DP
    placed = (
        P("section", tokens, None, None),
        P("section", tokens, None),
        P(None, DP),
        P("section", tokens, None),
        P("section", tokens, None),
        P(tokens),
        P("expert", None, DP),
        P("section", "expert", DP, None),
    )
    return jax.shard_map(
        on_device,
        mesh=finer,
        in_specs=placed,
        out_specs=P(("expert", "section"), DP),
        check_vma=False,
    )
```

```python
import jax
import jax.numpy as jnp
from jax import lax
from jax.experimental import pallas as pl
from jax.experimental.pallas import tpu as pltpu
from jax.sharding import PartitionSpec as P

SEQS = 64
CAP = 16
LANES = 128
ROOM = 20 << 20
F32 = jnp.float32
BF16 = jnp.bfloat16
DP = ("y_hi", "y_lo", "core")
CLOSE = ("y_lo", "core")
VMEM = pl.BlockSpec(memory_space=pltpu.VMEM)
SMEM = pl.BlockSpec(memory_space=pltpu.SMEM)


def exchange(x, axes):
    return lax.all_to_all(x, axes, split_axis=0, concat_axis=0, tiled=True)


def dot(a, b, contract=((1,), (0,)), **kw):
    return lax.dot_general(a, b, (contract, ((), ())), preferred_element_type=F32, **kw)


def iota(shape, axis):
    return lax.broadcasted_iota(jnp.int32, shape, axis)


def call(kernel, name, shape, dtype, *args):
    specs = [SMEM if a.ndim == 1 else VMEM for a in args]
    return pl.pallas_call(
        kernel,
        name=name,
        out_shape=jax.ShapeDtypeStruct(shape, dtype),
        in_specs=specs,
        out_specs=VMEM,
        compiler_params=pltpu.CompilerParams(vmem_limit_bytes=ROOM),
    )(*args)


def pack_kernel(acts_ref, grads_ref, routes_ref, out_ref):
    holders, _, chunk = out_ref.shape
    pairs = acts_ref.shape[0]
    toks, feats = grads_ref.shape
    width = feats // holders
    half = toks // 2
    token, lane = iota((toks, LANES), 0), iota((toks, LANES), 1) % pairs
    named = routes_ref[...].astype(F32).astype(BF16)
    first = dot(named, (lane == 2 * token).astype(F32).astype(BF16))
    second = dot(named, (lane == 2 * token + 1).astype(F32).astype(BF16))
    code = jnp.broadcast_to(first[0:1] + second[1:2], (toks, LANES))
    low = iota((toks, LANES), 1) < width % LANES
    for j in range(holders):
        out_ref[j, :pairs, :] = acts_ref[:, j * chunk : (j + 1) * chunk]
        base = width * j // LANES * LANES
        left = grads_ref[:, base : base + LANES]
        right = grads_ref[:, base + LANES : base + 2 * LANES]
        if width * j == base:
            right = jnp.where(low, right.astype(F32), code).astype(BF16)
        else:
            left = jnp.where(low, code, left.astype(F32)).astype(BF16)
        for k in range(2):
            rows = slice(k * half, (k + 1) * half)
            out_ref[j, pairs:, 2 * k * LANES : (2 * k + 1) * LANES] = left[rows]
            out_ref[j, pairs:, (2 * k + 1) * LANES : (2 * k + 2) * LANES] = right[rows]


def project_kernel(odd_ref, order_ref, got_ref, weights_ref, model_ref, out_ref):
    holders, rows, chunk = got_ref.shape
    rank = LANES // 2
    pairs = rank
    half = pairs // 2
    experts = weights_ref.shape[0] // rank
    odd = odd_ref[0] == 1
    low = iota((half, LANES), 1) < rank
    left = got_ref[:, pairs, 0:LANES].astype(F32)
    right = got_ref[:, pairs, LANES : 2 * LANES].astype(F32)
    code = jnp.where(odd, left, pltpu.roll(right, rank, 1))
    code = jnp.transpose(code)
    lane = iota((1, LANES), 1)
    wanted = [
        jnp.where(lane < rank, order_ref[2 * m], order_ref[2 * m + 1]).astype(F32) for m in range(experts // 2)
    ]
    part = 4
    for g in range(0, holders, part):
        every = dot(
            got_ref[g : g + part, :pairs, :].reshape(part * pairs, chunk), weights_ref[...], ((1,), (1,))
        )
        for h in range(part):
            col = jnp.broadcast_to(code[:pairs, g + h : g + h + 1], (pairs, LANES))
            own = jnp.zeros((pairs, LANES), F32)
            for m in range(experts // 2):
                block = every[h * pairs : (h + 1) * pairs, m * LANES : (m + 1) * LANES]
                own = own + jnp.where(col == wanted[m], block, 0.0)
            own = own + pltpu.roll(own, rank, 1)
            out_ref[g + h, :half, :] = jnp.where(low, own[:half], own[half:])
    side = rows - pairs
    begin = dot(got_ref[:, pairs:, : chunk // 2].reshape(holders * side, chunk // 2), model_ref[...], ((1,), (1,)))
    end = dot(got_ref[:, pairs:, chunk // 2 :].reshape(holders * side, chunk // 2), model_ref[...], ((1,), (1,)))
    both = jnp.where(iota((holders * side, LANES), 1) < rank, begin, end)
    out_ref[:, half:, :] = both.reshape(holders, side, LANES)


def slots_kernel(parts_ref, weight_ref, pick_ref, line_ref, out_ref):
    holders, rows, _ = parts_ref.shape
    experts = out_ref.shape[0]
    rank = LANES // 2
    toks = weight_ref.shape[0]
    whole = parts_ref[0]
    for h in range(1, holders):
        whole = whole + parts_ref[h]
    low = iota((toks, LANES), 1) < rank
    acts, dy = whole[:toks], whole[toks:]
    dy = jnp.concatenate([pltpu.roll(dy, rank, 1), dy], axis=0)
    table = jnp.concatenate(
        [
            jnp.where(low, acts, 0.0),
            jnp.where(low, pltpu.roll(acts, rank, 1), 0.0),
            jnp.where(low, 0.0, weight_ref[:, 0:1] * dy),
            jnp.where(low, 0.0, weight_ref[:, 1:2] * dy),
        ],
        axis=0,
    )
    slots = dot(pick_ref[...], table.astype(BF16)).astype(BF16)
    first = iota((experts, 8, LANES), 1) == 0
    line = jnp.where(first, line_ref[...][:, None, :], 0.0).astype(BF16)
    for i in range(out_ref.shape[1]):
        out_ref[:, i, :CAP, :] = slots.reshape(experts, CAP, LANES)
        out_ref[:, i, CAP:, :] = line


def score_kernel(mine_ref, known_ref, *refs):
    *q_refs, out_ref, sums_ref = refs
    blocks, rows, lanes = known_ref.shape
    rank, wide = q_refs[0].shape
    queries = wide // rank
    per = lanes // queries
    near = len(q_refs)
    experts, _, lines, _ = out_ref.shape
    spread_row, spread_col = iota((rank, lanes), 0), iota((rank, lanes), 1) // queries
    blank = jnp.zeros((rank, lanes), BF16)
    lhs = known_ref[:, :CAP, :].reshape(blocks * CAP, lanes)
    for c in range(wide // lanes):
        spread = (spread_row == c * per + spread_col).astype(F32).astype(BF16)
        under = jnp.concatenate([blank, spread], axis=1)
        for k in range(near):
            top = jnp.concatenate([q_refs[k][:, c * lanes : (c + 1) * lanes], blank], axis=1)
            both = dot(lhs, jnp.concatenate([top, under], axis=0))
            prod = both[:, :lanes] * both[:, lanes:]
            if c == 0:
                sums_ref[k] = prod
            else:
                sums_ref[k] += prod
    group = lanes // CAP
    own = iota((group, lanes), 1) // CAP == iota((group, lanes), 0)
    label = iota((SEQS, lanes), 0).astype(F32)
    sel = []
    for g in range(0, blocks, group):
        line = known_ref[g : g + group, CAP, :].astype(F32)
        seqs = jnp.sum(jnp.where(own, line, 0.0), axis=0, keepdims=True)
        sel.append((label == seqs).astype(F32).astype(BF16))
    sel = jnp.concatenate(sel, axis=1)
    scores = []
    for k in range(near):
        sums = sums_ref[k]
        high = sums.astype(BF16)
        low = (sums - high.astype(F32)).astype(BF16)
        total = dot(sel, jnp.concatenate([high, low], axis=1))
        score = total[:, :lanes] + total[:, lanes:]
        step = lanes // 2
        while step >= queries:
            score = score + pltpu.roll(score, step, 1)
            step //= 2
        scores.append(score[:, :queries])
    for i in range(near):
        part = scores[0]
        for k in range(1, near):
            part = jnp.where(mine_ref[0] == i ^ k, scores[k], part)
        out_ref[:, i, :, :] = part.reshape(experts, lines, queries)


def on_device(active, out_grad, proj_model, routes, route_weight, seq_ids, proj_hidden, query_feat):
    experts = lax.axis_size("expert")
    sections = lax.axis_size("section")
    holders = lax.axis_size(DP)
    far, near = lax.axis_size("y_hi"), lax.axis_size(CLOSE)
    toks, top, hidden = active.shape[1:]
    rank, width = proj_model.shape
    chunk = hidden // holders
    pairs = top * toks
    me = lax.axis_index("expert")
    odd = lax.axis_index("core")

    sent = call(
        pack_kernel, "pack", (holders, pairs + toks // 2, chunk), BF16,
        active[0].reshape(pairs, hidden), out_grad[0], routes[0].T,
    )
    got = exchange(sent, DP)

    weights = proj_hidden
    order = [0]
    bit = experts // 2
    while bit:
        other = lax.ppermute(weights, "expert", [(i, i ^ bit) for i in range(experts)])
        weights = jnp.concatenate([weights, other], axis=0)
        order = order + [o ^ bit for o in order]
        bit //= 2
    named = me ^ jnp.array(order, jnp.int32)
    gap = 2 * LANES - width
    model = jnp.where(
        odd == 1, jnp.pad(proj_model, ((0, 0), (gap, 0))), jnp.pad(proj_model, ((0, 0), (0, gap)))
    )
    model = jnp.concatenate([model, model], axis=0)
    partial = call(
        project_kernel, "project", (holders, toks + toks // 2, LANES), F32,
        odd.reshape(1), named, got, weights.reshape(experts * rank, chunk), model,
    )
    queries = query_feat.shape[2]
    q = query_feat[0, 0].reshape(queries, rank, rank).transpose(1, 2, 0).reshape(rank, rank * queries)
    partial, q = lax.optimization_barrier((partial, q))
    parts = exchange(partial, DP)

    ids = routes[0].reshape(pairs)
    member = (ids[:, None] == jnp.arange(experts)[None, :]).astype(BF16)
    before = dot(jnp.tril(jnp.ones((pairs, pairs), BF16), -1), member)
    place = jnp.sum(before * member.astype(F32), axis=1).astype(jnp.int32)
    slot = ids * CAP + place
    slot = jnp.concatenate([slot, slot.reshape(toks, top).T.reshape(pairs)])
    pick = (jnp.arange(experts * CAP)[:, None] == slot[None, :]).astype(BF16)
    belongs = (place[:, None] == (jnp.arange(LANES) % CAP)[None, :]).astype(BF16)
    pair_seq = jnp.repeat(seq_ids, top).astype(BF16)
    line = dot(member * pair_seq[:, None], belongs, ((0,), (0,)))
    slots = call(
        slots_kernel, "slots", (experts, far, CAP + 8, LANES), BF16, parts, route_weight[0], pick, line
    )
    near_q = [q] + [lax.ppermute(q, CLOSE, [(i, i ^ k) for i in range(near)]) for k in range(1, near)]
    slots, *near_q = lax.optimization_barrier((slots, *near_q))
    known = exchange(slots.reshape(experts * far, CAP + 8, LANES), ("expert", "y_hi"))

    lines = SEQS // experts
    scores = pl.pallas_call(
        score_kernel,
        name="score",
        out_shape=jax.ShapeDtypeStruct((experts, near, lines, queries), F32),
        in_specs=[SMEM] + [VMEM] * (1 + near),
        out_specs=VMEM,
        scratch_shapes=[pltpu.VMEM((near, experts * far * CAP, LANES), F32)],
        compiler_params=pltpu.CompilerParams(vmem_limit_bytes=ROOM),
    )(lax.axis_index(CLOSE).reshape(1), known, *near_q)
    out = exchange(
        scores.reshape(experts * near * sections, lines // sections, queries), ("expert",) + CLOSE + ("section",)
    )
    return jnp.sum(out, axis=0)


def solution(mesh):
    experts, holders, sections = mesh.devices.shape
    shape = (experts, holders // 4, 2, 2, sections)
    finer = jax.sharding.Mesh(mesh.devices.reshape(shape), ("expert",) + DP + ("section",))
    tokens = ("expert",) + DP
    placed = (
        P("section", tokens, None, None),
        P("section", tokens, None),
        P(None, DP),
        P("section", tokens, None),
        P("section", tokens, None),
        P(tokens),
        P("expert", None, DP),
        P("section", "expert", DP, None),
    )
    return jax.shard_map(
        on_device,
        mesh=finer,
        in_specs=placed,
        out_specs=P(("expert", "section"), DP),
        check_vma=False,
    )
```

```python
import jax
import jax.numpy as jnp
from jax import lax
from jax.experimental import pallas as pl
from jax.experimental.pallas import tpu as pltpu
from jax.sharding import PartitionSpec as P


SEQS = 64
CAP = 16
LANES = 128
ROOM = 20 << 20
F32 = jnp.float32
BF16 = jnp.bfloat16
DP = ("y_hi", "y_lo", "core")
CLOSE = ("y_lo", "core")
GROUP = ("y_lo", "core", "section")
VMEM = pl.BlockSpec(memory_space=pltpu.VMEM)
SMEM = pl.BlockSpec(memory_space=pltpu.SMEM)


def exchange(x, axes):
    return lax.all_to_all(x, axes, split_axis=0, concat_axis=0, tiled=True)


def dot(a, b, contract=((1,), (0,)), **kw):
    return lax.dot_general(a, b, (contract, ((), ())), preferred_element_type=F32, **kw)


def iota(shape, axis):
    return lax.broadcasted_iota(jnp.int32, shape, axis)


def call(kernel, shape, dtype, *args):
    specs = [SMEM if a.ndim == 1 else VMEM for a in args]
    return pl.pallas_call(
        kernel,
        out_shape=jax.ShapeDtypeStruct(shape, dtype),
        in_specs=specs,
        out_specs=VMEM,
        compiler_params=pltpu.CompilerParams(vmem_limit_bytes=ROOM),
    )(*args)


def pack_kernel(turn_ref, acts_ref, grads_ref, routes_ref, out_ref):
    holders, _, chunk = out_ref.shape
    pairs = acts_ref.shape[0]
    toks, feats = grads_ref.shape
    width = feats // holders
    half = toks // 2
    token, lane = iota((toks, LANES), 0), iota((toks, LANES), 1) % pairs
    named = routes_ref[...].astype(F32).astype(BF16)
    first = dot(named, (lane == 2 * token).astype(F32).astype(BF16))
    second = dot(named, (lane == 2 * token + 1).astype(F32).astype(BF16))
    code = jnp.broadcast_to(first[0:1] + second[1:2], (toks, LANES))
    low = iota((toks, LANES), 1) < width % LANES
    sections = 4
    spread = holders // sections
    for j in range(holders):
        place, section = j // sections, j % sections
        big = lax.rem(turn_ref[0] + section, sections)
        begin = pl.multiple_of(big * (spread * chunk) + place * chunk, chunk)
        out_ref[j, :pairs, :] = acts_ref[:, pl.ds(begin, chunk)]
        shift = width * place // LANES * LANES
        base = pl.multiple_of(big * (spread * width) + shift, LANES)
        left = grads_ref[:, pl.ds(base, LANES)]
        right = grads_ref[:, pl.ds(pl.multiple_of(base + LANES, LANES), LANES)]
        if width * place == shift:
            right = jnp.where(low, right.astype(F32), code).astype(BF16)
        else:
            left = jnp.where(low, code, left.astype(F32)).astype(BF16)
        for k in range(2):
            rows = slice(k * half, (k + 1) * half)
            out_ref[j, pairs:, 2 * k * LANES : (2 * k + 1) * LANES] = left[rows]
            out_ref[j, pairs:, (2 * k + 1) * LANES : (2 * k + 2) * LANES] = right[rows]


def project_kernel(odd_ref, order_ref, got_ref, weights_ref, model_ref, out_ref):
    holders, rows, chunk = got_ref.shape
    rank = LANES // 2
    pairs = rank
    half = pairs // 2
    experts = weights_ref.shape[0] // rank
    odd = odd_ref[0] == 1
    low = iota((half, LANES), 1) < rank
    left = got_ref[:, pairs, 0:LANES].astype(F32)
    right = got_ref[:, pairs, LANES : 2 * LANES].astype(F32)
    code = jnp.where(odd, left, pltpu.roll(right, rank, 1))
    code = jnp.transpose(code)
    lane = iota((1, LANES), 1)
    wanted = [
        jnp.where(lane < rank, order_ref[2 * m], order_ref[2 * m + 1]).astype(F32) for m in range(experts // 2)
    ]
    part = 4
    for g in range(0, holders, part):
        every = dot(
            got_ref[g : g + part, :pairs, :].reshape(part * pairs, chunk), weights_ref[...], ((1,), (1,))
        )
        for h in range(part):
            col = jnp.broadcast_to(code[:pairs, g + h : g + h + 1], (pairs, LANES))
            own = jnp.zeros((pairs, LANES), F32)
            for m in range(experts // 2):
                block = every[h * pairs : (h + 1) * pairs, m * LANES : (m + 1) * LANES]
                own = own + jnp.where(col == wanted[m], block, 0.0)
            own = own + pltpu.roll(own, rank, 1)
            out_ref[g + h, :half, :] = jnp.where(low, own[:half], own[half:])
    side = rows - pairs
    begin = dot(got_ref[:, pairs:, : chunk // 2].reshape(holders * side, chunk // 2), model_ref[...], ((1,), (1,)))
    end = dot(got_ref[:, pairs:, chunk // 2 :].reshape(holders * side, chunk // 2), model_ref[...], ((1,), (1,)))
    both = jnp.where(iota((holders * side, LANES), 1) < rank, begin, end)
    out_ref[:, half:, :] = both.reshape(holders, side, LANES)


def slots_kernel(parts_ref, weight_ref, pick_ref, line_ref, out_ref):
    holders, _, _ = parts_ref.shape
    experts = out_ref.shape[0]
    rank = LANES // 2
    toks = weight_ref.shape[0]
    whole = parts_ref[0]
    for h in range(1, holders):
        whole = whole + parts_ref[h]
    low = iota((toks, LANES), 1) < rank
    acts, dy = whole[:toks], whole[toks:]
    dy = jnp.concatenate([pltpu.roll(dy, rank, 1), dy], axis=0)
    table = jnp.concatenate(
        [
            jnp.where(low, acts, 0.0),
            jnp.where(low, pltpu.roll(acts, rank, 1), 0.0),
            jnp.where(low, 0.0, weight_ref[:, 0:1] * dy),
            jnp.where(low, 0.0, weight_ref[:, 1:2] * dy),
        ],
        axis=0,
    )
    slots = dot(pick_ref[...], table.astype(BF16)).astype(BF16)
    first = iota((experts, 8, LANES), 1) == 0
    line = jnp.where(first, line_ref[...][:, None, :], 0.0).astype(BF16)
    for i in range(out_ref.shape[1]):
        out_ref[:, i, :CAP, :] = slots.reshape(experts, CAP, LANES)
        out_ref[:, i, CAP:, :] = line


def score_kernel(mine_ref, known_ref, *refs):
    *q_refs, out_ref, sums_ref = refs
    blocks, _, lanes = known_ref.shape
    rank, wide = q_refs[0].shape
    queries = wide // rank
    per = lanes // queries
    near = len(q_refs)
    experts, _, lines, _ = out_ref.shape
    spread_row, spread_col = iota((rank, lanes), 0), iota((rank, lanes), 1) // queries
    blank = jnp.zeros((rank, lanes), BF16)
    lhs = known_ref[:, :CAP, :].reshape(blocks * CAP, lanes)
    for c in range(wide // lanes):
        spread = (spread_row == c * per + spread_col).astype(F32).astype(BF16)
        under = jnp.concatenate([blank, spread], axis=1)
        for k in range(near):
            top = jnp.concatenate([q_refs[k][:, c * lanes : (c + 1) * lanes], blank], axis=1)
            both = dot(lhs, jnp.concatenate([top, under], axis=0))
            prod = both[:, :lanes] * both[:, lanes:]
            if c == 0:
                sums_ref[k] = prod
            else:
                sums_ref[k] += prod
    group = lanes // CAP
    own = iota((group, lanes), 1) // CAP == iota((group, lanes), 0)
    label = iota((SEQS, lanes), 0).astype(F32)
    sel = []
    for g in range(0, blocks, group):
        line = known_ref[g : g + group, CAP, :].astype(F32)
        seqs = jnp.sum(jnp.where(own, line, 0.0), axis=0, keepdims=True)
        sel.append((label == seqs).astype(F32).astype(BF16))
    sel = jnp.concatenate(sel, axis=1)
    scores = []
    for k in range(near):
        sums = sums_ref[k]
        high = sums.astype(BF16)
        low = (sums - high.astype(F32)).astype(BF16)
        total = dot(sel, jnp.concatenate([high, low], axis=1))
        score = total[:, :lanes] + total[:, lanes:]
        step = lanes // 2
        while step >= queries:
            score = score + pltpu.roll(score, step, 1)
            step //= 2
        scores.append(score[:, :queries])
    for i in range(near):
        part = scores[0]
        for k in range(1, near):
            part = jnp.where(mine_ref[0] == i ^ k, scores[k], part)
        out_ref[:, i, :, :] = part.reshape(experts, lines, queries)


def scores_of(active, out_grad, proj_model, routes, route_weight, seq_ids, proj_hidden, query_feat):
    experts = lax.axis_size("expert")
    sections = lax.axis_size("section")
    holders = lax.axis_size(DP)
    far, near = lax.axis_size("y_hi"), lax.axis_size(CLOSE)
    toks, top, hidden = active.shape[1:]
    rank, width = proj_model.shape
    chunk = hidden // holders
    pairs = top * toks
    me = lax.axis_index("expert")
    odd = lax.axis_index("core")

    gap = 2 * LANES - width
    model = jnp.where(
        odd == 1, jnp.pad(proj_model, ((0, 0), (gap, 0))), jnp.pad(proj_model, ((0, 0), (0, gap)))
    )
    tied = jnp.concatenate([proj_hidden[0], model], axis=1)
    moves = [
        ((section + y) % far * sections + section, y * sections + section)
        for y in range(far)
        for section in range(sections)
    ]
    tied = lax.ppermute(tied, ("y_hi", "section"), moves)

    sent = call(
        pack_kernel, (holders, pairs + toks // 2, chunk), BF16,
        lax.axis_index("y_hi").reshape(1), active[0].reshape(pairs, hidden), out_grad[0], routes[0].T,
    )
    tied, sent = lax.optimization_barrier((tied, sent))
    got = exchange(sent, GROUP)

    weights, model = tied[None, :, :chunk], tied[:, chunk:]
    order = [0]
    bit = experts // 2
    while bit:
        other = lax.ppermute(weights, "expert", [(i, i ^ bit) for i in range(experts)])
        weights = jnp.concatenate([weights, other], axis=0)
        order = order + [o ^ bit for o in order]
        bit //= 2
    named = me ^ jnp.array(order, jnp.int32)
    model = jnp.concatenate([model, model], axis=0)
    partial = call(
        project_kernel, (holders, toks + toks // 2, LANES), F32,
        odd.reshape(1), named, got, weights.reshape(experts * rank, chunk), model,
    )
    queries = query_feat.shape[2]
    q = query_feat[0, 0].reshape(queries, rank, rank).transpose(1, 2, 0).reshape(rank, rank * queries)
    partial, q = lax.optimization_barrier((partial, q))
    parts = exchange(partial, GROUP)

    ids = routes[0].reshape(pairs)
    member = (ids[:, None] == jnp.arange(experts)[None, :]).astype(BF16)
    before = dot(jnp.tril(jnp.ones((pairs, pairs), BF16), -1), member)
    place = jnp.sum(before * member.astype(F32), axis=1).astype(jnp.int32)
    slot = ids * CAP + place
    slot = jnp.concatenate([slot, slot.reshape(toks, top).T.reshape(pairs)])
    pick = (jnp.arange(experts * CAP)[:, None] == slot[None, :]).astype(BF16)
    belongs = (place[:, None] == (jnp.arange(LANES) % CAP)[None, :]).astype(BF16)
    pair_seq = jnp.repeat(seq_ids, top).astype(BF16)
    line = dot(member * pair_seq[:, None], belongs, ((0,), (0,)))
    slots = call(slots_kernel, (experts, far, CAP + 8, LANES), BF16, parts, route_weight[0], pick, line)
    near_q = [q] + [lax.ppermute(q, CLOSE, [(i, i ^ k) for i in range(near)]) for k in range(1, near)]
    known = exchange(slots.reshape(experts * far, CAP + 8, LANES), ("expert", "y_hi"))

    lines = SEQS // experts
    scores = pl.pallas_call(
        score_kernel,
        name="score",
        out_shape=jax.ShapeDtypeStruct((experts, near, lines, queries), F32),
        in_specs=[SMEM] + [VMEM] * (1 + near),
        out_specs=VMEM,
        scratch_shapes=[pltpu.VMEM((near, experts * far * CAP, LANES), F32)],
        compiler_params=pltpu.CompilerParams(vmem_limit_bytes=ROOM),
    )(lax.axis_index(CLOSE).reshape(1), known, *near_q)
    out = exchange(
        scores.reshape(experts * near * sections, lines // sections, queries), ("expert",) + CLOSE + ("section",)
    )
    return jnp.sum(out, axis=0)


def solution(mesh):
    experts, holders, sections = mesh.devices.shape
    shape = (experts, holders // 4, 2, 2, sections)
    finer = jax.sharding.Mesh(mesh.devices.reshape(shape), ("expert",) + DP + ("section",))
    tokens = ("expert",) + DP
    placed = (
        P("section", tokens, None, None),
        P("section", tokens, None),
        P(None, DP),
        P("section", tokens, None),
        P("section", tokens, None),
        P(tokens),
        P("expert", None, DP),
        P("section", "expert", DP, None),
    )
    return jax.shard_map(
        scores_of,
        mesh=finer,
        in_specs=placed,
        out_specs=P(("expert", "section"), DP),
        check_vma=False,
    )
```

```python
import jax
import jax.numpy as jnp
from jax import lax
from jax.experimental import pallas as pl
from jax.experimental.pallas import tpu as pltpu
from jax.sharding import PartitionSpec as P


SEQS = 64
CAP = 16
LANES = 128
ROOM = 20 << 20
F32 = jnp.float32
BF16 = jnp.bfloat16
DP = ("y_hi", "y_lo", "core")
CLOSE = ("y_lo", "core")
GROUP = ("y_lo", "core", "section")
VMEM = pl.BlockSpec(memory_space=pltpu.VMEM)
SMEM = pl.BlockSpec(memory_space=pltpu.SMEM)


def exchange(x, axes):
    return lax.all_to_all(x, axes, split_axis=0, concat_axis=0, tiled=True)


def dot(a, b, contract=((1,), (0,)), **kw):
    return lax.dot_general(a, b, (contract, ((), ())), preferred_element_type=F32, **kw)


def iota(shape, axis):
    return lax.broadcasted_iota(jnp.int32, shape, axis)


def call(kernel, shape, dtype, *args):
    specs = [SMEM if a.ndim == 1 else VMEM for a in args]
    return pl.pallas_call(
        kernel,
        out_shape=jax.ShapeDtypeStruct(shape, dtype),
        in_specs=specs,
        out_specs=VMEM,
        compiler_params=pltpu.CompilerParams(vmem_limit_bytes=ROOM),
    )(*args)


def pack_kernel(turn_ref, acts_ref, grads_ref, routes_ref, out_ref):
    holders, _, chunk = out_ref.shape
    pairs = acts_ref.shape[0]
    toks, feats = grads_ref.shape
    width = feats // holders
    half = toks // 2
    token, lane = iota((toks, LANES), 0), iota((toks, LANES), 1) % pairs
    named = routes_ref[...].astype(F32).astype(BF16)
    first = dot(named, (lane == 2 * token).astype(F32).astype(BF16))
    second = dot(named, (lane == 2 * token + 1).astype(F32).astype(BF16))
    code = jnp.broadcast_to(first[0:1] + second[1:2], (toks, LANES))
    low = iota((toks, LANES), 1) < width % LANES
    sections = 4
    spread = holders // sections
    for j in range(holders):
        place, section = j // sections, j % sections
        big = lax.rem(turn_ref[0] + (section + 2 * (place % 2)) % sections, sections)
        begin = pl.multiple_of(big * (spread * chunk) + place * chunk, chunk)
        out_ref[j, :pairs, :] = acts_ref[:, pl.ds(begin, chunk)]
        shift = width * place // LANES * LANES
        base = pl.multiple_of(big * (spread * width) + shift, LANES)
        left = grads_ref[:, pl.ds(base, LANES)]
        right = grads_ref[:, pl.ds(pl.multiple_of(base + LANES, LANES), LANES)]
        if width * place == shift:
            right = jnp.where(low, right.astype(F32), code).astype(BF16)
        else:
            left = jnp.where(low, code, left.astype(F32)).astype(BF16)
        for k in range(2):
            rows = slice(k * half, (k + 1) * half)
            out_ref[j, pairs:, 2 * k * LANES : (2 * k + 1) * LANES] = left[rows]
            out_ref[j, pairs:, (2 * k + 1) * LANES : (2 * k + 2) * LANES] = right[rows]


def project_kernel(odd_ref, order_ref, got_ref, weights_ref, model_ref, out_ref):
    holders, rows, chunk = got_ref.shape
    rank = LANES // 2
    pairs = rank
    half = pairs // 2
    experts = weights_ref.shape[0] // rank
    odd = odd_ref[0] == 1
    low = iota((half, LANES), 1) < rank
    left = got_ref[:, pairs, 0:LANES].astype(F32)
    right = got_ref[:, pairs, LANES : 2 * LANES].astype(F32)
    code = jnp.where(odd, left, pltpu.roll(right, rank, 1))
    code = jnp.transpose(code)
    lane = iota((1, LANES), 1)
    wanted = [
        jnp.where(lane < rank, order_ref[2 * m], order_ref[2 * m + 1]).astype(F32) for m in range(experts // 2)
    ]
    part = 4
    for g in range(0, holders, part):
        every = dot(
            got_ref[g : g + part, :pairs, :].reshape(part * pairs, chunk), weights_ref[...], ((1,), (1,))
        )
        for h in range(part):
            col = jnp.broadcast_to(code[:pairs, g + h : g + h + 1], (pairs, LANES))
            own = jnp.zeros((pairs, LANES), F32)
            for m in range(experts // 2):
                block = every[h * pairs : (h + 1) * pairs, m * LANES : (m + 1) * LANES]
                own = own + jnp.where(col == wanted[m], block, 0.0)
            own = own + pltpu.roll(own, rank, 1)
            out_ref[g + h, :half, :] = jnp.where(low, own[:half], own[half:])
    side = rows - pairs
    begin = dot(got_ref[:, pairs:, : chunk // 2].reshape(holders * side, chunk // 2), model_ref[...], ((1,), (1,)))
    end = dot(got_ref[:, pairs:, chunk // 2 :].reshape(holders * side, chunk // 2), model_ref[...], ((1,), (1,)))
    both = jnp.where(iota((holders * side, LANES), 1) < rank, begin, end)
    out_ref[:, half:, :] = both.reshape(holders, side, LANES)


def slots_kernel(parts_ref, weight_ref, pick_ref, line_ref, out_ref):
    holders, _, _ = parts_ref.shape
    experts = out_ref.shape[0]
    rank = LANES // 2
    toks = weight_ref.shape[0]
    whole = parts_ref[0]
    for h in range(1, holders):
        whole = whole + parts_ref[h]
    low = iota((toks, LANES), 1) < rank
    acts, dy = whole[:toks], whole[toks:]
    dy = jnp.concatenate([pltpu.roll(dy, rank, 1), dy], axis=0)
    table = jnp.concatenate(
        [
            jnp.where(low, acts, 0.0),
            jnp.where(low, pltpu.roll(acts, rank, 1), 0.0),
            jnp.where(low, 0.0, weight_ref[:, 0:1] * dy),
            jnp.where(low, 0.0, weight_ref[:, 1:2] * dy),
        ],
        axis=0,
    )
    slots = dot(pick_ref[...], table.astype(BF16)).astype(BF16)
    first = iota((experts, 8, LANES), 1) == 0
    line = jnp.where(first, line_ref[...][:, None, :], 0.0).astype(BF16)
    for i in range(out_ref.shape[1]):
        out_ref[:, i, :CAP, :] = slots.reshape(experts, CAP, LANES)
        out_ref[:, i, CAP:, :] = line


def score_kernel(mine_ref, known_ref, *refs):
    *q_refs, out_ref, sums_ref = refs
    blocks, _, lanes = known_ref.shape
    rank, wide = q_refs[0].shape
    queries = wide // rank
    per = lanes // queries
    near = len(q_refs)
    experts, _, lines, _ = out_ref.shape
    spread_row, spread_col = iota((rank, lanes), 0), iota((rank, lanes), 1) // queries
    blank = jnp.zeros((rank, lanes), BF16)
    lhs = known_ref[:, :CAP, :].reshape(blocks * CAP, lanes)
    for c in range(wide // lanes):
        spread = (spread_row == c * per + spread_col).astype(F32).astype(BF16)
        under = jnp.concatenate([blank, spread], axis=1)
        for k in range(near):
            top = jnp.concatenate([q_refs[k][:, c * lanes : (c + 1) * lanes], blank], axis=1)
            both = dot(lhs, jnp.concatenate([top, under], axis=0))
            prod = both[:, :lanes] * both[:, lanes:]
            if c == 0:
                sums_ref[k] = prod
            else:
                sums_ref[k] += prod
    group = lanes // CAP
    own = iota((group, lanes), 1) // CAP == iota((group, lanes), 0)
    label = iota((SEQS, lanes), 0).astype(F32)
    sel = []
    for g in range(0, blocks, group):
        line = known_ref[g : g + group, CAP, :].astype(F32)
        seqs = jnp.sum(jnp.where(own, line, 0.0), axis=0, keepdims=True)
        sel.append((label == seqs).astype(F32).astype(BF16))
    sel = jnp.concatenate(sel, axis=1)
    scores = []
    for k in range(near):
        sums = sums_ref[k]
        high = sums.astype(BF16)
        low = (sums - high.astype(F32)).astype(BF16)
        total = dot(sel, jnp.concatenate([high, low], axis=1))
        score = total[:, :lanes] + total[:, lanes:]
        step = lanes // 2
        while step >= queries:
            score = score + pltpu.roll(score, step, 1)
            step //= 2
        scores.append(score[:, :queries])
    for i in range(near):
        part = scores[0]
        for k in range(1, near):
            part = jnp.where(mine_ref[0] == i ^ k, scores[k], part)
        out_ref[:, i, :, :] = part.reshape(experts, lines, queries)


def scores_of(active, out_grad, proj_model, routes, route_weight, seq_ids, proj_hidden, query_feat):
    experts = lax.axis_size("expert")
    sections = lax.axis_size("section")
    holders = lax.axis_size(DP)
    far, near = lax.axis_size("y_hi"), lax.axis_size(CLOSE)
    toks, top, hidden = active.shape[1:]
    rank, width = proj_model.shape
    chunk = hidden // holders
    pairs = top * toks
    me = lax.axis_index("expert")
    odd = lax.axis_index("core")

    gap = 2 * LANES - width
    model = jnp.where(
        odd == 1, jnp.pad(proj_model, ((0, 0), (gap, 0))), jnp.pad(proj_model, ((0, 0), (0, gap)))
    )
    tied = jnp.concatenate([proj_hidden[0], model], axis=1)
    cores = lax.axis_size("core")
    seats = [(y, core, section) for y in range(far) for core in range(cores) for section in range(sections)]
    moves = [
        (((section + 2 * core + y) % far * cores + core) * sections + section, (y * cores + core) * sections + section)
        for y, core, section in seats
    ]
    span = len(seats)
    across = [
        ((e ^ experts // 2) * span + source, e * span + target) for e in range(experts) for source, target in moves
    ]
    weights = lax.ppermute(tied, ("y_hi", "core", "section"), moves)
    other = lax.ppermute(proj_hidden, ("expert", "y_hi", "core", "section"), across)

    sent = call(
        pack_kernel, (holders, pairs + toks // 2, chunk), BF16,
        lax.axis_index("y_hi").reshape(1), active[0].reshape(pairs, hidden), out_grad[0], routes[0].T,
    )
    got = exchange(sent, GROUP)

    weights, model = weights[None, :, :chunk], weights[:, chunk:]
    weights = jnp.concatenate([weights, other], axis=0)
    order = [0, experts // 2]
    bit = experts // 4
    while bit:
        other = lax.ppermute(weights, "expert", [(i, i ^ bit) for i in range(experts)])
        weights = jnp.concatenate([weights, other], axis=0)
        order = order + [o ^ bit for o in order]
        bit //= 2
    named = me ^ jnp.array(order, jnp.int32)
    model = jnp.concatenate([model, model], axis=0)
    partial = call(
        project_kernel, (holders, toks + toks // 2, LANES), F32,
        odd.reshape(1), named, got, weights.reshape(experts * rank, chunk), model,
    )
    queries = query_feat.shape[2]
    q = query_feat[0, 0].reshape(queries, rank, rank).transpose(1, 2, 0).reshape(rank, rank * queries)
    partial, q = lax.optimization_barrier((partial, q))
    parts = exchange(partial, GROUP)

    ids = routes[0].reshape(pairs)
    member = (ids[:, None] == jnp.arange(experts)[None, :]).astype(BF16)
    before = dot(jnp.tril(jnp.ones((pairs, pairs), BF16), -1), member)
    place = jnp.sum(before * member.astype(F32), axis=1).astype(jnp.int32)
    slot = ids * CAP + place
    slot = jnp.concatenate([slot, slot.reshape(toks, top).T.reshape(pairs)])
    pick = (jnp.arange(experts * CAP)[:, None] == slot[None, :]).astype(BF16)
    belongs = (place[:, None] == (jnp.arange(LANES) % CAP)[None, :]).astype(BF16)
    pair_seq = jnp.repeat(seq_ids, top).astype(BF16)
    line = dot(member * pair_seq[:, None], belongs, ((0,), (0,)))
    slots = call(slots_kernel, (experts, 1, CAP + 8, LANES), BF16, parts, route_weight[0], pick, line)
    near_q = [q] + [lax.ppermute(q, CLOSE, [(i, i ^ k) for i in range(near)]) for k in range(1, near)]
    moved = exchange(slots.reshape(experts, CAP + 8, LANES), "expert")
    copies = jnp.broadcast_to(moved[None], (far,) + moved.shape)
    known = exchange(copies.reshape((far * experts,) + moved.shape[1:]), "y_hi")

    lines = SEQS // experts
    scores = pl.pallas_call(
        score_kernel,
        name="score",
        out_shape=jax.ShapeDtypeStruct((experts, near, lines, queries), F32),
        in_specs=[SMEM] + [VMEM] * (1 + near),
        out_specs=VMEM,
        scratch_shapes=[pltpu.VMEM((near, experts * far * CAP, LANES), F32)],
        compiler_params=pltpu.CompilerParams(vmem_limit_bytes=ROOM),
    )(lax.axis_index(CLOSE).reshape(1), known, *near_q)
    out = exchange(
        scores.reshape(experts * near * sections, lines // sections, queries), ("expert",) + CLOSE + ("section",)
    )
    return jnp.sum(out, axis=0)


def solution(mesh):
    experts, holders, sections = mesh.devices.shape
    shape = (experts, holders // 4, 2, 2, sections)
    finer = jax.sharding.Mesh(mesh.devices.reshape(shape), ("expert",) + DP + ("section",))
    tokens = ("expert",) + DP
    placed = (
        P("section", tokens, None, None),
        P("section", tokens, None),
        P(None, DP),
        P("section", tokens, None),
        P("section", tokens, None),
        P(tokens),
        P("expert", None, DP),
        P("section", "expert", DP, None),
    )
    return jax.shard_map(
        scores_of,
        mesh=finer,
        in_specs=placed,
        out_specs=P(("expert", "section"), DP),
        check_vma=False,
    )
```

```python
import jax
import jax.numpy as jnp
from jax import lax
from jax.experimental import pallas as pl
from jax.experimental.pallas import tpu as pltpu
from jax.sharding import PartitionSpec as P


SEQS = 64
CAP = 16
LANES = 128
ROOM = 20 << 20
F32 = jnp.float32
BF16 = jnp.bfloat16
DP = ("y_hi", "y_lo", "core")
CLOSE = ("y_lo", "core")
GROUP = ("y_lo", "core", "section")
VMEM = pl.BlockSpec(memory_space=pltpu.VMEM)
SMEM = pl.BlockSpec(memory_space=pltpu.SMEM)


def exchange(x, axes):
    return lax.all_to_all(x, axes, split_axis=0, concat_axis=0, tiled=True)


def dot(a, b, contract=((1,), (0,)), **kw):
    return lax.dot_general(a, b, (contract, ((), ())), preferred_element_type=F32, **kw)


def iota(shape, axis):
    return lax.broadcasted_iota(jnp.int32, shape, axis)


def call(kernel, shape, dtype, *args):
    specs = [SMEM if a.ndim == 1 else VMEM for a in args]
    return pl.pallas_call(
        kernel,
        out_shape=jax.ShapeDtypeStruct(shape, dtype),
        in_specs=specs,
        out_specs=VMEM,
        compiler_params=pltpu.CompilerParams(vmem_limit_bytes=ROOM),
    )(*args)


def pack_kernel(turn_ref, acts_ref, grads_ref, routes_ref, out_ref):
    holders, _, chunk = out_ref.shape
    pairs = acts_ref.shape[0]
    toks, feats = grads_ref.shape
    width = feats // holders
    half = toks // 2
    token, lane = iota((toks, LANES), 0), iota((toks, LANES), 1) % pairs
    named = routes_ref[...].astype(F32).astype(BF16)
    first = dot(named, (lane == 2 * token).astype(F32).astype(BF16))
    second = dot(named, (lane == 2 * token + 1).astype(F32).astype(BF16))
    code = jnp.broadcast_to(first[0:1] + second[1:2], (toks, LANES))
    low = iota((toks, LANES), 1) < width % LANES
    sections = 4
    spread = holders // sections
    for j in range(holders):
        place, section = j // sections, j % sections
        big = lax.rem(turn_ref[0] + (section + 2 * (place % 2)) % sections, sections)
        begin = pl.multiple_of(big * (spread * chunk) + place * chunk, chunk)
        out_ref[j, :pairs, :] = acts_ref[:, pl.ds(begin, chunk)]
        shift = width * place // LANES * LANES
        base = pl.multiple_of(big * (spread * width) + shift, LANES)
        left = grads_ref[:, pl.ds(base, LANES)]
        right = grads_ref[:, pl.ds(pl.multiple_of(base + LANES, LANES), LANES)]
        if width * place == shift:
            right = jnp.where(low, right.astype(F32), code).astype(BF16)
        else:
            left = jnp.where(low, code, left.astype(F32)).astype(BF16)
        for k in range(2):
            rows = slice(k * half, (k + 1) * half)
            out_ref[j, pairs:, 2 * k * LANES : (2 * k + 1) * LANES] = left[rows]
            out_ref[j, pairs:, (2 * k + 1) * LANES : (2 * k + 2) * LANES] = right[rows]


def project_kernel(odd_ref, order_ref, got_ref, weights_ref, model_ref, out_ref):
    holders, rows, chunk = got_ref.shape
    rank = LANES // 2
    pairs = rank
    half = pairs // 2
    experts = weights_ref.shape[0] // rank
    odd = odd_ref[0] == 1
    low = iota((half, LANES), 1) < rank
    left = got_ref[:, pairs, 0:LANES].astype(F32)
    right = got_ref[:, pairs, LANES : 2 * LANES].astype(F32)
    code = jnp.where(odd, left, pltpu.roll(right, rank, 1))
    code = jnp.transpose(code)
    lane = iota((1, LANES), 1)
    wanted = [
        jnp.where(lane < rank, order_ref[2 * m], order_ref[2 * m + 1]).astype(F32) for m in range(experts // 2)
    ]
    part = 4
    for g in range(0, holders, part):
        every = dot(
            got_ref[g : g + part, :pairs, :].reshape(part * pairs, chunk), weights_ref[...], ((1,), (1,))
        )
        for h in range(part):
            col = jnp.broadcast_to(code[:pairs, g + h : g + h + 1], (pairs, LANES))
            own = jnp.zeros((pairs, LANES), F32)
            for m in range(experts // 2):
                block = every[h * pairs : (h + 1) * pairs, m * LANES : (m + 1) * LANES]
                own = own + jnp.where(col == wanted[m], block, 0.0)
            own = own + pltpu.roll(own, rank, 1)
            out_ref[g + h, :half, :] = jnp.where(low, own[:half], own[half:])
    side = rows - pairs
    begin = dot(got_ref[:, pairs:, : chunk // 2].reshape(holders * side, chunk // 2), model_ref[...], ((1,), (1,)))
    end = dot(got_ref[:, pairs:, chunk // 2 :].reshape(holders * side, chunk // 2), model_ref[...], ((1,), (1,)))
    both = jnp.where(iota((holders * side, LANES), 1) < rank, begin, end)
    out_ref[:, half:, :] = both.reshape(holders, side, LANES)


def slots_kernel(parts_ref, weight_ref, pick_ref, line_ref, out_ref):
    holders, _, _ = parts_ref.shape
    experts = out_ref.shape[0]
    rank = LANES // 2
    toks = weight_ref.shape[0]
    whole = parts_ref[0]
    for h in range(1, holders):
        whole = whole + parts_ref[h]
    low = iota((toks, LANES), 1) < rank
    acts, dy = whole[:toks], whole[toks:]
    dy = jnp.concatenate([pltpu.roll(dy, rank, 1), dy], axis=0)
    table = jnp.concatenate(
        [
            jnp.where(low, acts, 0.0),
            jnp.where(low, pltpu.roll(acts, rank, 1), 0.0),
            jnp.where(low, 0.0, weight_ref[:, 0:1] * dy),
            jnp.where(low, 0.0, weight_ref[:, 1:2] * dy),
        ],
        axis=0,
    )
    slots = dot(pick_ref[...], table.astype(BF16)).astype(BF16)
    first = iota((experts, 8, LANES), 1) == 0
    line = jnp.where(first, line_ref[...][:, None, :], 0.0).astype(BF16)
    for i in range(out_ref.shape[1]):
        out_ref[:, i, :CAP, :] = slots.reshape(experts, CAP, LANES)
        out_ref[:, i, CAP:, :] = line


def score_kernel(mine_ref, known_ref, *refs):
    *q_refs, out_ref, sums_ref = refs
    blocks, _, lanes = known_ref.shape
    rank, wide = q_refs[0].shape
    queries = wide // rank
    per = lanes // queries
    near = len(q_refs)
    experts, _, lines, _ = out_ref.shape
    spread_row, spread_col = iota((rank, lanes), 0), iota((rank, lanes), 1) // queries
    blank = jnp.zeros((rank, lanes), BF16)
    lhs = known_ref[:, :CAP, :].reshape(blocks * CAP, lanes)
    for c in range(wide // lanes):
        spread = (spread_row == c * per + spread_col).astype(F32).astype(BF16)
        under = jnp.concatenate([blank, spread], axis=1)
        for k in range(near):
            top = jnp.concatenate([q_refs[k][:, c * lanes : (c + 1) * lanes], blank], axis=1)
            both = dot(lhs, jnp.concatenate([top, under], axis=0))
            prod = both[:, :lanes] * both[:, lanes:]
            if c == 0:
                sums_ref[k] = prod
            else:
                sums_ref[k] += prod
    group = lanes // CAP
    own = iota((group, lanes), 1) // CAP == iota((group, lanes), 0)
    label = iota((SEQS, lanes), 0).astype(F32)
    sel = []
    for g in range(0, blocks, group):
        line = known_ref[g : g + group, CAP, :].astype(F32)
        seqs = jnp.sum(jnp.where(own, line, 0.0), axis=0, keepdims=True)
        sel.append((label == seqs).astype(F32).astype(BF16))
    sel = jnp.concatenate(sel, axis=1)
    scores = []
    for k in range(near):
        sums = sums_ref[k]
        high = sums.astype(BF16)
        low = (sums - high.astype(F32)).astype(BF16)
        total = dot(sel, jnp.concatenate([high, low], axis=1))
        score = total[:, :lanes] + total[:, lanes:]
        step = lanes // 2
        while step >= queries:
            score = score + pltpu.roll(score, step, 1)
            step //= 2
        scores.append(score[:, :queries])
    for i in range(near):
        part = scores[0]
        for k in range(1, near):
            part = jnp.where(mine_ref[0] == i ^ k, scores[k], part)
        out_ref[:, i, :, :] = part.reshape(experts, lines, queries)


def scores_of(active, out_grad, proj_model, routes, route_weight, seq_ids, proj_hidden, query_feat):
    experts = lax.axis_size("expert")
    sections = lax.axis_size("section")
    holders = lax.axis_size(DP)
    far, near = lax.axis_size("y_hi"), lax.axis_size(CLOSE)
    toks, top, hidden = active.shape[1:]
    rank, width = proj_model.shape
    chunk = hidden // holders
    pairs = top * toks
    me = lax.axis_index("expert")
    odd = lax.axis_index("core")

    cores = lax.axis_size("core")
    seats = [(y, core, section) for y in range(far) for core in range(cores) for section in range(sections)]
    moves = [
        (((section + 2 * core + y) % far * cores + core) * sections + section, (y * cores + core) * sections + section)
        for y, core, section in seats
    ]
    span = len(seats)
    across = [
        ((e ^ experts // 2) * span + source, e * span + target) for e in range(experts) for source, target in moves
    ]
    weights = lax.ppermute(proj_hidden, ("y_hi", "core", "section"), moves)
    other = lax.ppermute(proj_hidden, ("expert", "y_hi", "core", "section"), across)

    sent = call(
        pack_kernel, (holders, pairs + toks // 2, chunk), BF16,
        lax.axis_index("y_hi").reshape(1), active[0].reshape(pairs, hidden), out_grad[0], routes[0].T,
    )
    got = exchange(sent, GROUP)

    weights = jnp.concatenate([weights, other], axis=0)
    order = [0, experts // 2]
    bit = experts // 4
    while bit:
        other = lax.ppermute(weights, "expert", [(i, i ^ bit) for i in range(experts)])
        weights = jnp.concatenate([weights, other], axis=0)
        order = order + [o ^ bit for o in order]
        bit //= 2
    gap = 2 * LANES - width
    model = jnp.where(
        odd == 1, jnp.pad(proj_model, ((0, 0), (gap, 0))), jnp.pad(proj_model, ((0, 0), (0, gap)))
    )
    model = lax.ppermute(model, ("y_hi", "core", "section"), moves)
    named = me ^ jnp.array(order, jnp.int32)
    model = jnp.concatenate([model, model], axis=0)
    partial = call(
        project_kernel, (holders, toks + toks // 2, LANES), F32,
        odd.reshape(1), named, got, weights.reshape(experts * rank, chunk), model,
    )
    queries = query_feat.shape[2]
    q = query_feat[0, 0].reshape(queries, rank, rank).transpose(1, 2, 0).reshape(rank, rank * queries)
    partial, q = lax.optimization_barrier((partial, q))
    parts = exchange(partial, GROUP)

    ids = routes[0].reshape(pairs)
    member = (ids[:, None] == jnp.arange(experts)[None, :]).astype(BF16)
    before = dot(jnp.tril(jnp.ones((pairs, pairs), BF16), -1), member)
    place = jnp.sum(before * member.astype(F32), axis=1).astype(jnp.int32)
    slot = ids * CAP + place
    slot = jnp.concatenate([slot, slot.reshape(toks, top).T.reshape(pairs)])
    pick = (jnp.arange(experts * CAP)[:, None] == slot[None, :]).astype(BF16)
    belongs = (place[:, None] == (jnp.arange(LANES) % CAP)[None, :]).astype(BF16)
    pair_seq = jnp.repeat(seq_ids, top).astype(BF16)
    line = dot(member * pair_seq[:, None], belongs, ((0,), (0,)))
    slots = call(slots_kernel, (experts, far, CAP + 8, LANES), BF16, parts, route_weight[0], pick, line)
    near_q = [q] + [lax.ppermute(q, CLOSE, [(i, i ^ k) for i in range(near)]) for k in range(1, near)]
    known = exchange(slots.reshape(experts * far, CAP + 8, LANES), ("expert", "y_hi"))

    lines = SEQS // experts
    scores = pl.pallas_call(
        score_kernel,
        name="score",
        out_shape=jax.ShapeDtypeStruct((experts, near, lines, queries), F32),
        in_specs=[SMEM] + [VMEM] * (1 + near),
        out_specs=VMEM,
        scratch_shapes=[pltpu.VMEM((near, experts * far * CAP, LANES), F32)],
        compiler_params=pltpu.CompilerParams(vmem_limit_bytes=ROOM),
    )(lax.axis_index(CLOSE).reshape(1), known, *near_q)
    out = exchange(
        scores.reshape(experts * near * sections, lines // sections, queries), ("expert",) + CLOSE + ("section",)
    )
    return jnp.sum(out, axis=0)


def solution(mesh):
    experts, holders, sections = mesh.devices.shape
    shape = (experts, holders // 4, 2, 2, sections)
    finer = jax.sharding.Mesh(mesh.devices.reshape(shape), ("expert",) + DP + ("section",))
    tokens = ("expert",) + DP
    placed = (
        P("section", tokens, None, None),
        P("section", tokens, None),
        P(None, DP),
        P("section", tokens, None),
        P("section", tokens, None),
        P(tokens),
        P("expert", None, DP),
        P("section", "expert", DP, None),
    )
    return jax.shard_map(
        scores_of,
        mesh=finer,
        in_specs=placed,
        out_specs=P(("expert", "section"), DP),
        check_vma=False,
    )
```

```python
import functools

import jax
import jax.numpy as jnp
from jax import lax
from jax.experimental import pallas as pl
from jax.experimental.pallas import tpu as pltpu
from jax.sharding import PartitionSpec as P


SEQS = 64
CAP = 16
LANES = 128
ROOM = 20 << 20
F32 = jnp.float32
BF16 = jnp.bfloat16
DP = ("y_hi", "y_lo", "core")
CLOSE = ("y_lo", "core")
GROUP = ("y_lo", "core", "section")
VMEM = pl.BlockSpec(memory_space=pltpu.VMEM)
SMEM = pl.BlockSpec(memory_space=pltpu.SMEM)


def exchange(x, axes):
    return lax.all_to_all(x, axes, split_axis=0, concat_axis=0, tiled=True)


def dot(a, b, contract=((1,), (0,)), **kw):
    return lax.dot_general(a, b, (contract, ((), ())), preferred_element_type=F32, **kw)


def iota(shape, axis):
    return lax.broadcasted_iota(jnp.int32, shape, axis)


def call(kernel, shape, dtype, *args):
    specs = [SMEM if a.ndim == 1 else VMEM for a in args]
    return pl.pallas_call(
        kernel,
        out_shape=jax.ShapeDtypeStruct(shape, dtype),
        in_specs=specs,
        out_specs=VMEM,
        compiler_params=pltpu.CompilerParams(vmem_limit_bytes=ROOM),
    )(*args)


def pack_kernel(turn_ref, acts_ref, grads_ref, routes_ref, out_ref):
    holders, _, chunk = out_ref.shape
    pairs = acts_ref.shape[0]
    toks, feats = grads_ref.shape
    width = feats // holders
    half = toks // 2
    token, lane = iota((toks, LANES), 0), iota((toks, LANES), 1) % pairs
    named = routes_ref[...].astype(F32).astype(BF16)
    first = dot(named, (lane == 2 * token).astype(F32).astype(BF16))
    second = dot(named, (lane == 2 * token + 1).astype(F32).astype(BF16))
    code = jnp.broadcast_to(first[0:1] + second[1:2], (toks, LANES))
    low = iota((toks, LANES), 1) < width % LANES
    sections = 4
    spread = holders // sections
    for j in range(holders):
        place, section = j // sections, j % sections
        big = lax.rem(turn_ref[0] + (section + 2 * (place % 2)) % sections, sections)
        begin = pl.multiple_of(big * (spread * chunk) + place * chunk, chunk)
        out_ref[j, :pairs, :] = acts_ref[:, pl.ds(begin, chunk)]
        shift = width * place // LANES * LANES
        base = pl.multiple_of(big * (spread * width) + shift, LANES)
        left = grads_ref[:, pl.ds(base, LANES)]
        right = grads_ref[:, pl.ds(pl.multiple_of(base + LANES, LANES), LANES)]
        if width * place == shift:
            right = jnp.where(low, right.astype(F32), code).astype(BF16)
        else:
            left = jnp.where(low, code, left.astype(F32)).astype(BF16)
        for k in range(2):
            rows = slice(k * half, (k + 1) * half)
            out_ref[j, pairs:, 2 * k * LANES : (2 * k + 1) * LANES] = left[rows]
            out_ref[j, pairs:, (2 * k + 1) * LANES : (2 * k + 2) * LANES] = right[rows]


def project_kernel(first, odd_ref, order_ref, got_ref, weights_ref, rest_ref, out_ref):
    holders, rows, chunk = got_ref.shape
    rank = LANES // 2
    pairs = rank
    half = pairs // 2
    experts = weights_ref.shape[0] // rank
    odd = odd_ref[0] == 1
    low = iota((half, LANES), 1) < rank
    left = got_ref[:, pairs, 0:LANES].astype(F32)
    right = got_ref[:, pairs, LANES : 2 * LANES].astype(F32)
    code = jnp.where(odd, left, pltpu.roll(right, rank, 1))
    code = jnp.transpose(code)
    lane = iota((1, LANES), 1)
    wanted = [
        jnp.where(lane < rank, order_ref[2 * m], order_ref[2 * m + 1]).astype(F32) for m in range(experts // 2)
    ]
    part = 4
    for g in range(0, holders, part):
        every = dot(
            got_ref[g : g + part, :pairs, :].reshape(part * pairs, chunk), weights_ref[...], ((1,), (1,))
        )
        for h in range(part):
            col = jnp.broadcast_to(code[:pairs, g + h : g + h + 1], (pairs, LANES))
            own = jnp.zeros((pairs, LANES), F32)
            for m in range(experts // 2):
                block = every[h * pairs : (h + 1) * pairs, m * LANES : (m + 1) * LANES]
                own = own + jnp.where(col == wanted[m], block, 0.0)
            own = own + pltpu.roll(own, rank, 1)
            own = jnp.where(low, own[:half], own[half:])
            out_ref[g + h, :half, :] = own if first else own + rest_ref[g + h, :half, :]
    if not first:
        out_ref[:, half:, :] = rest_ref[:, half:, :]
        return
    side = rows - pairs
    begin = dot(got_ref[:, pairs:, : chunk // 2].reshape(holders * side, chunk // 2), rest_ref[...], ((1,), (1,)))
    end = dot(got_ref[:, pairs:, chunk // 2 :].reshape(holders * side, chunk // 2), rest_ref[...], ((1,), (1,)))
    both = jnp.where(iota((holders * side, LANES), 1) < rank, begin, end)
    out_ref[:, half:, :] = both.reshape(holders, side, LANES)


def slots_kernel(parts_ref, weight_ref, pick_ref, line_ref, out_ref):
    holders, _, _ = parts_ref.shape
    experts = out_ref.shape[0]
    rank = LANES // 2
    toks = weight_ref.shape[0]
    whole = parts_ref[0]
    for h in range(1, holders):
        whole = whole + parts_ref[h]
    low = iota((toks, LANES), 1) < rank
    acts, dy = whole[:toks], whole[toks:]
    dy = jnp.concatenate([pltpu.roll(dy, rank, 1), dy], axis=0)
    table = jnp.concatenate(
        [
            jnp.where(low, acts, 0.0),
            jnp.where(low, pltpu.roll(acts, rank, 1), 0.0),
            jnp.where(low, 0.0, weight_ref[:, 0:1] * dy),
            jnp.where(low, 0.0, weight_ref[:, 1:2] * dy),
        ],
        axis=0,
    )
    slots = dot(pick_ref[...], table.astype(BF16)).astype(BF16)
    first = iota((experts, 8, LANES), 1) == 0
    line = jnp.where(first, line_ref[...][:, None, :], 0.0).astype(BF16)
    for i in range(out_ref.shape[1]):
        out_ref[:, i, :CAP, :] = slots.reshape(experts, CAP, LANES)
        out_ref[:, i, CAP:, :] = line


def score_kernel(mine_ref, known_ref, *refs):
    *q_refs, out_ref, sums_ref = refs
    blocks, _, lanes = known_ref.shape
    rank, wide = q_refs[0].shape
    queries = wide // rank
    per = lanes // queries
    near = len(q_refs)
    experts, _, lines, _ = out_ref.shape
    spread_row, spread_col = iota((rank, lanes), 0), iota((rank, lanes), 1) // queries
    blank = jnp.zeros((rank, lanes), BF16)
    lhs = known_ref[:, :CAP, :].reshape(blocks * CAP, lanes)
    for c in range(wide // lanes):
        spread = (spread_row == c * per + spread_col).astype(F32).astype(BF16)
        under = jnp.concatenate([blank, spread], axis=1)
        for k in range(near):
            top = jnp.concatenate([q_refs[k][:, c * lanes : (c + 1) * lanes], blank], axis=1)
            both = dot(lhs, jnp.concatenate([top, under], axis=0))
            prod = both[:, :lanes] * both[:, lanes:]
            if c == 0:
                sums_ref[k] = prod
            else:
                sums_ref[k] += prod
    group = lanes // CAP
    own = iota((group, lanes), 1) // CAP == iota((group, lanes), 0)
    row = iota((SEQS, lanes), 0)
    label = (row % (SEQS // 2) * 2 + row // (SEQS // 2)).astype(F32)
    sel = []
    for g in range(0, blocks, group):
        line = known_ref[g : g + group, CAP, :].astype(F32)
        seqs = jnp.sum(jnp.where(own, line, 0.0), axis=0, keepdims=True)
        sel.append((label == seqs).astype(F32).astype(BF16))
    sel = jnp.concatenate(sel, axis=1)
    scores = []
    for k in range(near):
        sums = sums_ref[k]
        high = sums.astype(BF16)
        low = (sums - high.astype(F32)).astype(BF16)
        total = dot(sel, jnp.concatenate([high, low], axis=1))
        score = total[:, :lanes] + total[:, lanes:]
        step = lanes // 2
        while step >= queries:
            score = score + pltpu.roll(score, step, 1)
            step //= 2
        first = iota((SEQS // 2, lanes), 1) < queries
        scores.append(jnp.where(first, score[: SEQS // 2], score[SEQS // 2 :])[:, : 2 * queries])
    for i in range(near):
        part = scores[0]
        for k in range(1, near):
            part = jnp.where(mine_ref[0] == i ^ k, scores[k], part)
        out_ref[:, i, :, :] = part.reshape(experts, lines, 2 * queries)


def scores_of(active, out_grad, proj_model, routes, route_weight, seq_ids, proj_hidden, query_feat):
    experts = lax.axis_size("expert")
    sections = lax.axis_size("section")
    holders = lax.axis_size(DP)
    far, near = lax.axis_size("y_hi"), lax.axis_size(CLOSE)
    toks, top, hidden = active.shape[1:]
    rank, width = proj_model.shape
    chunk = hidden // holders
    pairs = top * toks
    me = lax.axis_index("expert")
    odd = lax.axis_index("core")

    cores = lax.axis_size("core")
    seats = [(y, core, section) for y in range(far) for core in range(cores) for section in range(sections)]
    moves = [
        (((section + 2 * core + y) % far * cores + core) * sections + section, (y * cores + core) * sections + section)
        for y, core, section in seats
    ]
    span = len(seats)
    across = [
        ((e ^ experts // 2) * span + source, e * span + target) for e in range(experts) for source, target in moves
    ]
    weights = lax.ppermute(proj_hidden, ("y_hi", "core", "section"), moves)
    other = lax.ppermute(proj_hidden, ("expert", "y_hi", "core", "section"), across)

    sent = call(
        pack_kernel, (holders, pairs + toks // 2, chunk), BF16,
        lax.axis_index("y_hi").reshape(1), active[0].reshape(pairs, hidden), out_grad[0], routes[0].T,
    )
    got = exchange(sent, GROUP)

    weights = jnp.concatenate([weights, other], axis=0)
    order = [0, experts // 2]
    bit = experts // 4
    while bit > 1:
        other = lax.ppermute(weights, "expert", [(i, i ^ bit) for i in range(experts)])
        weights = jnp.concatenate([weights, other], axis=0)
        order = order + [o ^ bit for o in order]
        bit //= 2
    gap = 2 * LANES - width
    model = jnp.where(
        odd == 1, jnp.pad(proj_model, ((0, 0), (gap, 0))), jnp.pad(proj_model, ((0, 0), (0, gap)))
    )
    model = lax.ppermute(model, ("y_hi", "core", "section"), moves)
    other = lax.ppermute(weights, "expert", [(i, i ^ 1) for i in range(experts)])
    named = me ^ jnp.array(order, jnp.int32)
    model = jnp.concatenate([model, model], axis=0)
    shape = (holders, toks + toks // 2, LANES)
    partial = call(
        functools.partial(project_kernel, True), shape, F32,
        odd.reshape(1), named, got, weights.reshape(-1, chunk), model,
    )
    partial = call(
        functools.partial(project_kernel, False), shape, F32,
        odd.reshape(1), named ^ 1, got, other.reshape(-1, chunk), partial,
    )
    queries = query_feat.shape[2]
    q = query_feat[0, 0].reshape(queries, rank, rank).transpose(1, 2, 0).reshape(rank, rank * queries)
    partial, q = lax.optimization_barrier((partial, q))
    parts = exchange(partial, GROUP)

    ids = routes[0].reshape(pairs)
    member = (ids[:, None] == jnp.arange(experts)[None, :]).astype(BF16)
    before = dot(jnp.tril(jnp.ones((pairs, pairs), BF16), -1), member)
    place = jnp.sum(before * member.astype(F32), axis=1).astype(jnp.int32)
    slot = ids * CAP + place
    slot = jnp.concatenate([slot, slot.reshape(toks, top).T.reshape(pairs)])
    pick = (jnp.arange(experts * CAP)[:, None] == slot[None, :]).astype(BF16)
    belongs = (place[:, None] == (jnp.arange(LANES) % CAP)[None, :]).astype(BF16)
    pair_seq = jnp.repeat(seq_ids, top).astype(BF16)
    line = dot(member * pair_seq[:, None], belongs, ((0,), (0,)))
    slots = call(slots_kernel, (experts, far, CAP + 8, LANES), BF16, parts, route_weight[0], pick, line)
    near_q = [q]
    for k in range(1, near):
        near_q.append(lax.ppermute(q, CLOSE, [(i, i ^ k) for i in range(near)]))
    known = exchange(slots.reshape(experts * far, CAP + 8, LANES), ("expert", "y_hi"))

    lines = SEQS // experts // 2
    scores = pl.pallas_call(
        score_kernel,
        name="score",
        out_shape=jax.ShapeDtypeStruct((experts, near, lines, 2 * queries), F32),
        in_specs=[SMEM] + [VMEM] * (1 + near),
        out_specs=VMEM,
        scratch_shapes=[pltpu.VMEM((near, experts * far * CAP, LANES), F32)],
        compiler_params=pltpu.CompilerParams(vmem_limit_bytes=ROOM),
    )(lax.axis_index(CLOSE).reshape(1), known, *near_q)
    out = exchange(scores.reshape(experts * near * lines, 1, 2 * queries), ("expert",) + CLOSE + ("section",))
    return jnp.sum(out, axis=0).reshape(2, queries)


def solution(mesh):
    experts, holders, sections = mesh.devices.shape
    shape = (experts, holders // 4, 2, 2, sections)
    finer = jax.sharding.Mesh(mesh.devices.reshape(shape), ("expert",) + DP + ("section",))
    tokens = ("expert",) + DP
    placed = (
        P("section", tokens, None, None),
        P("section", tokens, None),
        P(None, DP),
        P("section", tokens, None),
        P("section", tokens, None),
        P(tokens),
        P("expert", None, DP),
        P("section", "expert", DP, None),
    )
    return jax.shard_map(
        scores_of,
        mesh=finer,
        in_specs=placed,
        out_specs=P(("expert", "section"), DP),
        check_vma=False,
    )
```
